256 devices in a mesh: blk: 4 (over z_hi, core), grp: 64 (over y, z_lo, x).
Axes of the slice: x: 4, y: 4, z: 8 (z_hi: 2, z_lo: 4; z = z_hi * 4 + z_lo), core: 2. Of those that a mesh axis runs over, the one named last changes fastest.
Arguments:
- design: float32 [8, 32768], P(None, ('blk', 'grp')), may hold values from -5 to 5
- lengthscales: float32 [8], replicated, may hold values from 0.55 to 0.85
- counts: int32 [32768], P(('blk', 'grp')), may hold values from 1 to 16
- noise_base: float32 [1], replicated, may hold values from 0.5 to 2
- targets: float32 [16, 32768], P(None, ('blk', 'grp')), may hold values from -6 to 6
Outputs:
- solution: float32 [16, 32768], P(None, ('blk', 'grp'))
- residual: float32 [16, 32768], P(None, ('blk', 'grp'))
- image: float32 [16, 32768], P(None, ('blk', 'grp'))
The draws below stay inside these ranges and needn't reach their ends.
All inputs are finite; a program needn't handle non-finite values.
Results may differ from the reference program's by a relative error of at most 0.0003.
Values sent between devices are 32-bit elements; how exact they have to be, the bound alone decides.
A program may use at most 64 MiB of HBM per device.

```python
import math
import jax
import jax.numpy as jnp
from jax import lax

DIM = 8
NRHS = 16
N = 32768


def place_ends(array, own_key, smallest, top_value):
    place = [jax.random.randint(jax.random.fold_in(own_key, axis), (), 0, length) for axis, length in enumerate(array.shape)]
    widest = array.shape.index(max(array.shape))
    neighbour = place[:widest] + [(place[widest] + 1) % array.shape[widest]] + place[widest + 1:]
    return array.at[tuple(place)].set(smallest).at[tuple(neighbour)].set(top_value)


def shard_levels(rng, extent, split, low, high):
    def one(dim, blocks):
        steps = jax.random.uniform(jax.random.fold_in(jax.random.fold_in(rng, 6), dim), (blocks,), jnp.float32, low / len(split), high / len(split))
        return jnp.repeat(jnp.exp(steps), extent[dim] // blocks).reshape((-1,) + (1,) * (len(extent) - dim - 1))

    loudness = one(*split[0])
    for cut in split[1:]:
        loudness = loudness * one(*cut)
    return loudness


def gaussian(own_key, shape, spread, bound, shards=(), kind=jnp.bfloat16):
    result = jax.random.normal(own_key, shape, jnp.float32) * spread
    if len(shards) > 0:
        result = shard_levels(own_key, shape, shards, -0.22, 0.18) * result
    return jnp.clip(result, min=-bound, max=bound).astype(kind)


def setup_inputs(seed: int = 0) -> dict:
    seeds = jax.random.split(jax.random.key(seed), 6)
    return {
        "design": gaussian(seeds[0], (DIM, N), 1.0, 5.0, ((1, 256),), jnp.float32),
        "lengthscales": jnp.clip(jnp.exp(jax.random.uniform(seeds[1], (DIM,), jnp.float32, math.log(0.55), math.log(0.85))), 0.55, 0.85),
        "counts": place_ends(jax.random.randint(seeds[2], (N,), 1, 17), jax.random.fold_in(seeds[2], 1), 1, 16).astype(jnp.int32),
        "noise_base": jnp.clip(jnp.exp(jax.random.uniform(seeds[3], (1,), jnp.float32, math.log(0.5), math.log(2.0))), 0.5, 2.0),
        "targets": gaussian(seeds[4], (NRHS, N), 1.0, 6.0, ((1, 256),), jnp.float32),
    }


ROOT_FIVE = 2.23606797749979

def kernel_terms(own_scaled, own_square, col_scaled, col_dirs, running):
    columns = col_scaled.shape[1]
    block_width = math.gcd(columns, 2048)
    block_count = columns // block_width

    def advance(block_index, partial_sum):
        offset = block_index * block_width
        chosen = lax.dynamic_slice_in_dim(col_scaled, offset, block_width, 1)
        chosen_dirs = lax.dynamic_slice_in_dim(col_dirs, offset, block_width, 1)
        chosen_square = lax.optimization_barrier(jnp.sum(chosen * chosen, 0))
        inner_products = jnp.einsum('dr,dc->rc', own_scaled, chosen, precision=lax.Precision.HIGHEST)
        dist_square = jnp.maximum(own_square[:, None] + chosen_square[None, :] - 2.0 * inner_products, 0.0)
        radius = jnp.sqrt(dist_square)
        kernel_tile = (1.0 + ROOT_FIVE * radius + 5.0 / 3.0 * dist_square) * jnp.exp(-ROOT_FIVE * radius)
        return partial_sum + jnp.einsum('kc,rc->kr', chosen_dirs, kernel_tile, precision=lax.Precision.HIGHEST)
    return lax.fori_loop(0, block_count, advance, running)

def operator_apply(scaled, squares, noise_diag, direction):
    total_rows = scaled.shape[1]
    row_width = math.gcd(total_rows, 512)
    row_count = total_rows // row_width

    def one_block(block_index):
        offset = (block_index * row_width).astype(jnp.int32)
        own = lax.dynamic_slice_in_dim(scaled, offset, row_width, 1)
        own_sq = lax.dynamic_slice_in_dim(squares, offset, row_width, 0)
        zero_start = jnp.zeros((direction.shape[0], row_width), jnp.float32)
        return kernel_terms(own, own_sq, scaled, direction, zero_start)
    blocks = lax.map(one_block, jnp.arange(row_count, dtype=jnp.int32))
    product_sum = jnp.transpose(blocks, (1, 0, 2)).reshape(direction.shape)
    return product_sum + noise_diag[None, :] * direction

def reference(design, lengthscales, counts, noise_base, targets):
    scaled = design / lengthscales[:, None]
    squares = lax.optimization_barrier(jnp.sum(scaled * scaled, 0))
    noise_diag = noise_base[0] / counts.astype(jnp.float32)
    first = operator_apply(scaled, squares, noise_diag, targets)
    gammas = lax.optimization_barrier(jnp.sum(targets * targets, 1))
    deltas = lax.optimization_barrier(jnp.sum(first * targets, 1))
    further = operator_apply(scaled, squares, noise_diag, first)
    alphas = (gammas / deltas)[:, None]
    solution = alphas * targets
    residual = targets - alphas * first
    image = first - alphas * further
    return (solution, residual, image)
```

```python
import functools

import jax
import jax.numpy as jnp
from jax import lax
from jax.experimental import pallas as pl
from jax.experimental.pallas import tpu as pltpu
from jax.sharding import PartitionSpec as P

MESH = pl.DeviceIdType.MESH
F32, BF16 = jnp.float32, jnp.bfloat16

NRHS = 16
CH = 128
SCALE = 2.23606797749979 * 1.4426950408889634
QUAD = 0.6931471805599453**2 / 3.0
LIN = 0.6931471805599453 / QUAD
ONE = 1.0 / QUAD
TINY = 1e-30

COLS = ((0, 0), (0, 2), (2, 0), (2, 2), (0, 1), (1, 0), (1, 1), (1, 3), (1, 2), (2, 1), (0, 3), (3, 0), (3, 3), (3, 1), (3, 2), (2, 3))
ROWS = ((0, 0), (0, 1), (4, 0), (4, 1), (1, 0), (7, 1), (2, 0), (6, 1), (3, 0), (5, 1))
NC, NR = len(COLS), len(ROWS)
HALF = 10
TILE = 256


def hops(offset, sizes):
    return sum(min(d, s - d) for d, s in zip(offset, sizes))


COL_ORDER = sorted(range(1, NC), key=lambda s: -hops(COLS[s], (4, 4)))
ROW_ORDER = sorted(range(1, NR), key=lambda s: -hops(ROWS[s], (8, 1)))


def three_parts(x):
    h = x.astype(BF16).astype(F32)
    m = (x - h).astype(BF16).astype(F32)
    return h, m, (x - h - m).astype(BF16).astype(F32)


def features(points, own):
    h, m, l = three_parts(points)
    qh, qm, ql = three_parts(jnp.sum(points * points, 0, keepdims=True))
    row = lax.broadcasted_iota(jnp.int32, points.shape, 0)
    first = 0 if own else 3
    q = jnp.where(row == first, qh, jnp.where(row == first + 1, qm, jnp.where(row == first + 2, ql, jnp.where(row < 6, 1.0, 0.0))))
    zero = jnp.zeros_like(points)
    if own:
        return jnp.concatenate([h, h, m, h, l, m, q, zero], 0)
    h, m, l = -2.0 * h, -2.0 * m, -2.0 * l
    return jnp.concatenate([h, m, h, l, h, m, q, zero], 0)


def kernel_values(d):
    d = jnp.maximum(d, TINY)
    u = d * lax.rsqrt(d)
    return (d + u * LIN + ONE) * jnp.exp2(-u)


def dot(a, b, ca, cb):
    return lax.dot_general(a, b, (((ca,), (cb,)), ((), ())), preferred_element_type=F32)


def folded(y):
    return y[:NRHS] + y[NRHS:]


def split32(v):
    h = v.astype(BF16)
    return jnp.concatenate([h, (v - h.astype(F32)).astype(BF16)], 0)


def cg_kernel(
    design_ref, scales_ref, counts_ref, noise_ref, targets_ref,
    sol_ref, res_ref, img_ref,
    pc, pr, vc2, vr2, txr, txc, rxr, rxc, tot, rtot,
    fa, fb, vc, vr, khi, klo, ycol, y1,
    lsem, pcs, pcr, prs, prr, vcs, vcr, vrs, vrr, txrs, rxrs, txcs, rxcs, tots, totr,
):
    blk, grp = lax.axis_index("blk"), lax.axis_index("grp")
    z, core = (blk // 2) * 4 + (grp // 4) % 4, blk % 2
    y, x = grp // 16, grp % 4

    def col_peer(slot, sign):
        dx, dy = COLS[slot]
        px, py = (x + (sign * dx) % 4) % 4, (y + (sign * dy) % 4) % 4
        return (blk, py * 16 + (z % 4) * 4 + px)

    def row_at(dz, dc):
        pz, pcore = (z + dz % 8) % 8, (core + dc) % 2
        return ((pz // 4) * 2 + pcore, y * 16 + (pz % 4) * 4 + x)

    def row_peer(slot, sign):
        dz, dc = ROWS[slot]
        return row_at(sign * dz, dc)

    others = [(dz, dc) for dz in range(8) for dc in range(2) if (dz, dc) != (0, 0)]

    local = [
        pltpu.make_async_copy(design_ref, pc.at[0, 0:8], lsem.at[0]),
        pltpu.make_async_copy(targets_ref, pc.at[0, 8:24], lsem.at[1]),
        pltpu.make_async_copy(design_ref, pr.at[0, 0:8], lsem.at[2]),
        pltpu.make_async_copy(targets_ref, pr.at[0, 8:24], lsem.at[3]),
    ]
    for c in local:
        c.start()

    barrier = pltpu.get_barrier_semaphore()
    for dz, dc in others:
        pl.semaphore_signal(barrier, inc=1, device_id=row_at(dz, dc), device_id_type=MESH)
    for slot in range(1, NC):
        pl.semaphore_signal(barrier, inc=1, device_id=col_peer(slot, 1), device_id_type=MESH)
    for c in local:
        c.wait()
    pl.semaphore_wait(barrier, len(others) + NC - 1)

    def remote(src, dst, ssem, rsem, peer):
        return pltpu.make_async_remote_copy(src_ref=src, dst_ref=dst, send_sem=ssem, recv_sem=rsem, device_id=peer, device_id_type=MESH)

    gather = [remote(pc.at[0], pc.at[s], pcs.at[s], pcr.at[s], col_peer(s, -1)) for s in COL_ORDER]
    gather += [remote(pc.at[0], pr.at[s], prs.at[s], prr.at[s], row_peer(s, -1)) for s in ROW_ORDER]
    for c in gather:
        c.start()

    lane8 = lax.broadcasted_iota(jnp.int32, (8, CH), 0)
    scales = jnp.zeros((8, CH), F32)
    for d in range(8):
        scales = jnp.where(lane8 == d, scales_ref[d], scales)
    noise = noise_ref[0] / counts_ref[...].astype(F32)

    for c in gather:
        c.wait()

    for s in range(NC):
        at = slice(s * CH, (s + 1) * CH)
        fb[:, at] = features(pc[s, 0:8] / scales * SCALE, False).astype(BF16)
        vc[:, at] = split32(pc[s, 8:24])
    for s in range(NR):
        at = slice(s * CH, (s + 1) * CH)
        fa[at, :] = features(pr[s, 0:8] / scales * SCALE, True).T.astype(BF16)
        vr[:, at] = split32(pr[s, 8:24])

    def tile(r, c, first_pass):
        rows, cols = slice(r, r + TILE), slice(c, c + TILE)
        if not first_pass:
            return khi[rows, cols], klo[rows, cols]
        k = kernel_values(dot(fa[rows, :], fb[:, cols], 1, 0))
        hi = k.astype(BF16)
        lo = (k - hi.astype(F32)).astype(BF16)
        khi[rows, cols] = hi
        klo[rows, cols] = lo
        return hi, lo

    def apply(first_pass, p):
        ycol[...] = jnp.zeros_like(ycol)
        sends = []
        for r0 in (2, 0, 8, 6, 4):
            half = r0 < 4
            r = r0 * CH
            rows = slice(r, r + TILE)
            yrow = jnp.zeros((NRHS, TILE), F32)
            for c in range(0, (HALF if half else NC) * CH, TILE):
                cols = slice(c, c + TILE)
                hi, lo = tile(r, c, first_pass)
                yrow += folded(dot(vc[:, cols], hi, 1, 1)) + dot(vc[0:NRHS, cols], lo, 1, 1)
                if not half or c >= 4 * CH:
                    ycol[:, cols] += folded(dot(vr[:, rows], hi, 1, 0)) + dot(vr[0:NRHS, rows], lo, 1, 0)
            for s in (r0, r0 + 1):
                txr[p, s] = yrow[:, (s - r0) * CH : (s - r0 + 1) * CH]
                if s:
                    c = remote(txr.at[p, s], rxr.at[p, s], txrs.at[p, s], rxrs.at[p, s], row_peer(s, 1))
                    c.start()
                    sends.append(c)
        for s in COL_ORDER:
            txc[p, s] = ycol[:, s * CH : (s + 1) * CH]
            c = remote(txc.at[p, s], rxc.at[p, s], txcs.at[p, s], rxcs.at[p, s], col_peer(s, 1))
            c.start()
            sends.append(c)
        total = txr[p, 0] + ycol[:, 0:CH]
        for c in sends:
            c.wait()
        for s in range(1, NR):
            total += rxr[p, s]
        for s in range(1, NC):
            total += rxc[p, s]
        return total * QUAD

    own = pc[0, 8:24]
    first = apply(True, 0) + noise * own

    lane = lax.broadcasted_iota(jnp.int32, (NRHS, CH), 1)
    sub = lax.broadcasted_iota(jnp.int32, (NRHS, CH), 0)
    gamma = jnp.sum(own * own, 1, keepdims=True)
    delta = jnp.sum(first * own, 1, keepdims=True)
    marked = jnp.where(lane == sub, gamma, 0.0) + jnp.where(lane == sub + NRHS, delta, 0.0)
    stats = jnp.sum(marked, 0, keepdims=True)

    y1[...] = first
    vc2[0, 0:16] = first
    vc2[0, 16:24] = jnp.broadcast_to(stats, (8, CH))
    vr2[0] = first
    gather = [remote(vc2.at[0], vc2.at[s], vcs.at[s], vcr.at[s], col_peer(s, -1)) for s in COL_ORDER]
    gather += [remote(vr2.at[0], vr2.at[s], vrs.at[s], vrr.at[s], row_peer(s, -1)) for s in ROW_ORDER]
    for c in gather:
        c.start()
    for c in gather:
        c.wait()

    group_stats = vc2[0, 16:24]
    for s in range(1, NC):
        group_stats += vc2[s, 16:24]
    tot[...] = group_stats
    exchange = [remote(tot, rtot.at[i], tots.at[i], totr.at[i], row_at(dz, dc)) for i, (dz, dc) in enumerate(others)]
    for c in exchange:
        c.start()

    for s in range(NC):
        vc[:, s * CH : (s + 1) * CH] = split32(vc2[s, 0:16])
    for s in range(NR):
        vr[:, s * CH : (s + 1) * CH] = split32(vr2[s])
    further = apply(False, 1) + noise * y1[...]

    for c in exchange:
        c.wait()
    for i in range(len(others)):
        group_stats += rtot[i]
    spread = jnp.broadcast_to(group_stats[0:1], (NRHS, CH))
    gammas = jnp.sum(jnp.where(lane == sub, spread, 0.0), 1, keepdims=True)
    deltas = jnp.sum(jnp.where(lane == sub + NRHS, spread, 0.0), 1, keepdims=True)
    alphas = gammas / deltas
    first = y1[...]
    sol_ref[...] = alphas * own
    res_ref[...] = own - alphas * first
    img_ref[...] = first - alphas * further


def on_device(design, lengthscales, counts, noise_base, targets):
    out = jax.ShapeDtypeStruct((NRHS, CH), F32)
    vmem, smem, anywhere = (pl.BlockSpec(memory_space=m) for m in (pltpu.VMEM, pltpu.SMEM, pl.ANY))
    dma = pltpu.SemaphoreType.DMA
    return pl.pallas_call(
        cg_kernel,
        out_shape=(out, out, out),
        in_specs=[anywhere, smem, vmem, smem, anywhere],
        out_specs=(vmem, vmem, vmem),
        scratch_shapes=[
            pltpu.VMEM((NC, 24, CH), F32),
            pltpu.VMEM((NR, 24, CH), F32),
            pltpu.VMEM((NC, 24, CH), F32),
            pltpu.VMEM((NR, NRHS, CH), F32),
            pltpu.VMEM((2, NR, NRHS, CH), F32),
            pltpu.VMEM((2, NC, NRHS, CH), F32),
            pltpu.VMEM((2, NR, NRHS, CH), F32),
            pltpu.VMEM((2, NC, NRHS, CH), F32),
            pltpu.VMEM((8, CH), F32),
            pltpu.VMEM((15, 8, CH), F32),
            pltpu.VMEM((NR * CH, 64), BF16),
            pltpu.VMEM((64, NC * CH), BF16),
            pltpu.VMEM((2 * NRHS, NC * CH), BF16),
            pltpu.VMEM((2 * NRHS, NR * CH), BF16),
            pltpu.VMEM((NR * CH, NC * CH), BF16),
            pltpu.VMEM((NR * CH, NC * CH), BF16),
            pltpu.VMEM((NRHS, NC * CH), F32),
            pltpu.VMEM((NRHS, CH), F32),
            dma((4,)),
            dma((NC,)), dma((NC,)), dma((NR,)), dma((NR,)),
            dma((NC,)), dma((NC,)), dma((NR,)), dma((NR,)),
            dma((2, NR)), dma((2, NR)), dma((2, NC)), dma((2, NC)),
            dma((15,)), dma((15,)),
        ],
        compiler_params=pltpu.CompilerParams(collective_id=0, has_side_effects=True, vmem_limit_bytes=48 << 20),
    )(design, lengthscales, counts.reshape(1, CH), noise_base, targets)


def solution(mesh):
    both = ("blk", "grp")
    placed = (P(None, both), P(), P(both), P(), P(None, both))
    out = P(None, both)
    return jax.shard_map(on_device, mesh=mesh, in_specs=placed, out_specs=(out, out, out), check_vma=False)
```

```python
import functools

import jax
import jax.numpy as jnp
from jax import lax
from jax.experimental import pallas as pl
from jax.experimental.pallas import tpu as pltpu
from jax.sharding import PartitionSpec as P

MESH = pl.DeviceIdType.MESH
F32, BF16 = jnp.float32, jnp.bfloat16

NRHS = 16
CH = 128
SCALE = 2.23606797749979 * 1.4426950408889634
QUAD = 0.6931471805599453**2 / 3.0
LIN = 0.6931471805599453 / QUAD
ONE = 1.0 / QUAD
TINY = 1e-30

COLS = ((2, 2), (2, 0), (1, 2), (2, 1), (1, 1), (1, 3), (0, 0), (0, 2), (0, 1), (1, 0), (0, 3), (3, 0), (3, 3), (3, 1), (3, 2), (2, 3))
ROWS = ((0, 0), (0, 1), (4, 0), (4, 1), (1, 0), (7, 1), (2, 0), (6, 1), (3, 0), (5, 1))
NC, NR = len(COLS), len(ROWS)
OWN = COLS.index((0, 0))
TILE = 2 * CH
SUB = 64
HALF = (0, 1, 2, 3, 4)
ONE_WAY = (0, 3)
ROW_PEERS = tuple(sorted(((dz, dc) for dz in range(8) for dc in range(2) if dz or dc), key=lambda o: -min(o[0], 8 - o[0])))


def hops(offset, sizes):
    return sum(min(d, s - d) for d, s in zip(offset, sizes))


COL_ORDER = sorted((s for s in range(NC) if s != OWN), key=lambda s: -hops(COLS[s], (4, 4)))
ROW_ORDER = sorted(range(1, NR), key=lambda s: -hops(ROWS[s], (8, 1)))


def three_parts(x):
    h = x.astype(BF16).astype(F32)
    m = (x - h).astype(BF16).astype(F32)
    return h, m, (x - h - m).astype(BF16).astype(F32)


def features(points, own):
    h, m, l = three_parts(points)
    qh, qm, ql = three_parts(jnp.sum(points * points, 0, keepdims=True))
    row = lax.broadcasted_iota(jnp.int32, points.shape, 0)
    first = 0 if own else 3
    q = jnp.where(row == first, qh, jnp.where(row == first + 1, qm, jnp.where(row == first + 2, ql, jnp.where(row < 6, 1.0, 0.0))))
    zero = jnp.zeros_like(points)
    if own:
        return jnp.concatenate([h, h, m, h, l, m, q, zero], 0)
    h, m, l = -2.0 * h, -2.0 * m, -2.0 * l
    return jnp.concatenate([h, m, h, l, h, m, q, zero], 0)


def kernel_values(d):
    d = jnp.maximum(d, TINY)
    u = d * lax.rsqrt(d)
    return (d + u * LIN + ONE) * jnp.exp2(-u)


def dot(a, b, ca, cb):
    return lax.dot_general(a, b, (((ca,), (cb,)), ((), ())), preferred_element_type=F32)


def folded(y):
    return y[:NRHS] + y[NRHS:]


def split32(v):
    h = v.astype(BF16)
    return jnp.concatenate([h, (v - h.astype(F32)).astype(BF16)], 0)


def cg_kernel(
    design_ref, scales_ref, counts_ref, noise_ref, targets_ref,
    alpha_ref, first_ref, further_ref,
    scales_sm, noise_sm, counts_vm,
    dcol, drow, tcol, trow, fcol, frow, stats, tot, mine,
    txr, txc, rxr, rxc,
    fa, fb, vc, vr, khi, klo, yrow, ycol,
    lsem, ssem, dcr, drr, tcr, trr, fcr, frr, rxs, sts,
):
    blk, grp = lax.axis_index("blk"), lax.axis_index("grp")
    zh, core = lax.div(blk, 2), lax.rem(blk, 2)
    y, zl, x = lax.div(grp, 16), lax.rem(lax.div(grp, 4), 4), lax.rem(grp, 4)
    xs = [lax.rem(x + d, 4) for d in range(4)]
    ys = [lax.rem(y + d, 4) * 16 + zl * 4 for d in range(4)]
    zs = [lax.rem(zh * 4 + zl + d, 8) for d in range(8)]
    zblk = [lax.div(v, 4) * 2 for v in zs]
    zgrp = [lax.rem(v, 4) * 4 + y * 16 + x for v in zs]
    cores = [core, 1 - core]

    def col_at(dx, dy):
        return (blk, ys[dy % 4] + xs[dx % 4])

    def row_at(dz, dc):
        return (zblk[dz % 8] + cores[dc], zgrp[dz % 8])

    def col_peer(slot, sign):
        return col_at(sign * COLS[slot][0], sign * COLS[slot][1])

    def row_peer(slot, sign):
        return row_at(sign * ROWS[slot][0], ROWS[slot][1])

    barrier = pltpu.get_barrier_semaphore()
    for s in COL_ORDER:
        pl.semaphore_signal(barrier, inc=1, device_id=col_peer(s, 1), device_id_type=MESH)
    for o in ROW_PEERS:
        pl.semaphore_signal(barrier, inc=1, device_id=row_at(*o), device_id_type=MESH)

    local = [
        pltpu.make_async_copy(src, dst, lsem.at[i])
        for i, (src, dst) in enumerate((
            (scales_ref, scales_sm), (noise_ref, noise_sm), (counts_ref, counts_vm),
            (design_ref, dcol.at[OWN]), (design_ref, drow.at[0]), (targets_ref, tcol.at[OWN]), (targets_ref, trow.at[0]),
        ))
    ]
    for c in local:
        c.start()
    pl.semaphore_wait(barrier, len(COL_ORDER) + len(ROW_PEERS))

    def remote(src, dst, ssem_at, rsem, peer):
        return pltpu.make_async_remote_copy(
            src_ref=src, dst_ref=dst, send_sem=ssem.at[ssem_at], recv_sem=rsem, device_id=peer, device_id_type=MESH
        )

    def gather(src, col, col_sem, row, row_sem, at):
        order = [(hops(COLS[s], (4, 4)), 0, s) for s in COL_ORDER] + [(hops(ROWS[s], (8, 1)), 1, s) for s in ROW_ORDER]
        for _, is_row, s in sorted(order, key=lambda o: -o[0]):
            if is_row:
                remote(src, row.at[s], at + 1, row_sem.at[s // 2], row_peer(s, -1)).start()
            else:
                remote(src, col.at[s], at, col_sem.at[s // 2], col_peer(s, -1)).start()

    def pair_wait(buf, sem, pair, own):
        lo, hi = 2 * pair, 2 * pair + 2
        lo = lo + 1 if lo == own else lo
        remote(buf.at[lo:hi], buf.at[lo:hi], 0, sem.at[pair], col_peer(0, 1)).wait_recv()

    def sent(ref, at):
        remote(ref, ref, at, rxs.at[0, 0], col_peer(0, 1)).wait_send()

    gather(design_ref, dcol, dcr, drow, drr, 0)
    gather(targets_ref, tcol, tcr, trow, trr, 2)

    for c in local:
        c.wait()
    dim = lax.broadcasted_iota(jnp.int32, (8, CH), 0)
    scales = jnp.zeros((8, CH), F32)
    for d in range(8):
        scales = jnp.where(dim == d, scales_sm[d], scales)
    noise = noise_sm[0] / counts_vm[...].astype(F32)
    yrow[...] = jnp.zeros_like(yrow)
    ycol[...] = jnp.zeros_like(ycol)
    have = set()

    def need(key, wait, use):
        if key not in have:
            have.add(key)
            wait()
            use()

    def col_points(p):
        def use():
            for s in (2 * p, 2 * p + 1):
                fb[p, :, (s - 2 * p) * CH : (s - 2 * p + 1) * CH] = features(dcol[s] / scales * SCALE, False).astype(BF16)

        need(("dc", p), lambda: pair_wait(dcol, dcr, p, OWN), use)

    def row_points(r):
        def use():
            for s in (2 * r, 2 * r + 1):
                fa[r, (s - 2 * r) * CH : (s - 2 * r + 1) * CH, :] = features(drow[s] / scales * SCALE, True).T.astype(BF16)

        need(("dr", r), lambda: pair_wait(drow, drr, r, 0), use)

    def vectors(key, buf, sem, pair, own, out):
        def use():
            for s in (2 * pair, 2 * pair + 1):
                out[pair, :, (s - 2 * pair) * CH : (s - 2 * pair + 1) * CH] = split32(buf[s])

        need((key, pair), lambda: pair_wait(buf, sem, pair, own), use)

    def tile(r, p):
        for q in range(0, TILE, SUB):
            k = kernel_values(dot(fa[r, q : q + SUB, :], fb[p], 1, 0))
            hi = k.astype(BF16)
            khi[r, p, q : q + SUB, :] = hi
            klo[r, p, q : q + SUB, :] = (k - hi.astype(F32)).astype(BF16)

    def to_rows(r, p):
        yrow[r] += folded(dot(vc[p], khi[r, p], 1, 1)) + dot(vc[p, 0:NRHS], klo[r, p], 1, 1)

    def to_cols(r, p):
        if r > 1 or p not in ONE_WAY:
            ycol[p] += folded(dot(vr[r], khi[r, p], 1, 0)) + dot(vr[r, 0:NRHS], klo[r, p], 1, 0)

    def send_row(k, r):
        for s in (2 * r, 2 * r + 1):
            if s:
                txr[k, s - 1] = yrow[r, :, (s - 2 * r) * CH : (s - 2 * r + 1) * CH]
                remote(txr.at[k, s - 1], rxr.at[k, s - 1], 4 + 2 * k, rxs.at[k, 0], row_peer(s, 1)).start()

    def send_col(k, p):
        for s in (2 * p, 2 * p + 1):
            if s != OWN:
                i = s - (s > OWN)
                txc[k, i] = ycol[p, :, (s - 2 * p) * CH : (s - 2 * p + 1) * CH]
                remote(txc.at[k, i], rxc.at[k, i], 5 + 2 * k, rxs.at[k, 1], col_peer(s, 1)).start()

    def total(k):
        own = yrow[0, :, 0:CH] + ycol[OWN // 2, :, (OWN % 2) * CH : (OWN % 2 + 1) * CH]
        remote(rxr.at[k], rxr.at[k], 0, rxs.at[k, 0], col_peer(0, 1)).wait_recv()
        for i in range(NR - 1):
            own += rxr[k, i]
        remote(rxc.at[k], rxc.at[k], 0, rxs.at[k, 1], col_peer(0, 1)).wait_recv()
        for i in range(NC - 1):
            own += rxc[k, i]
        return own * QUAD

    jobs = [(0, p) for p in (4, 3, 2, 1, 0)] + [(1, p) for p in (0, 1, 2, 3, 4)] + [(4, p) for p in range(8)]
    col_last = (0, 7, 1, 6, 2, 5, 3, 4)
    jobs += [(r, p) for p in col_last for r in (3, 2)]
    lag = 3
    for i in range(len(jobs) + lag):
        if i < len(jobs):
            r, p = jobs[i]
            row_points(r)
            col_points(p)
            tile(r, p)
        if i >= lag:
            r, p = jobs[i - lag]
            vectors("tc", tcol, tcr, p, OWN, vc)
            vectors("tr", trow, trr, r, 0, vr)
            to_rows(r, p)
            to_cols(r, p)
            if i - lag == 4:
                send_row(0, 0)
            if i - lag == 9:
                send_row(0, 1)
            if i - lag == 17:
                send_row(0, 4)
            if i - lag >= 18 and r == 2:
                send_col(0, p)
    send_row(0, 3)
    send_row(0, 2)

    sent(dcol.at[0 : NC - 1], 0)
    sent(drow.at[0 : NR - 1], 1)
    sent(tcol.at[0 : NC - 1], 2)
    sent(trow.at[0 : NR - 1], 3)
    own = tcol[OWN]
    lane = lax.broadcasted_iota(jnp.int32, (NRHS, CH), 1)
    sub = lax.broadcasted_iota(jnp.int32, (NRHS, CH), 0)
    gamma = jnp.sum(own * own, 1, keepdims=True)
    first = total(0) + noise * own

    fcol[OWN] = first
    frow[0] = first
    gather(fcol.at[OWN], fcol, fcr, frow, frr, 8)

    delta = jnp.sum(first * own, 1, keepdims=True)
    marked = jnp.where(lane == sub, gamma, 0.0) + jnp.where(lane == sub + NRHS, delta, 0.0)
    mine[0] = jnp.sum(marked, 0, keepdims=True)
    for s in COL_ORDER:
        remote(mine.at[0], stats.at[s - (s > OWN)], 10, sts.at[0], col_peer(s, 1)).start()
    first_ref[...] = first
    yrow[...] = jnp.zeros_like(yrow)
    ycol[...] = jnp.zeros_like(ycol)

    def from_row(r):
        vectors("fr", frow, frr, r, 0, vr)
        for p in HALF if r < 2 else range(8):
            to_cols(r, p)

    def from_col(p):
        vectors("fc", fcol, fcr, p, OWN, vc)
        for r in range(5) if p in HALF else (2, 3, 4):
            to_rows(r, p)

    from_row(0)
    from_col(4)
    from_col(5)
    from_row(2)
    from_col(3)
    from_col(2)
    from_col(6)
    from_row(3)
    from_col(1)
    from_col(7)
    from_col(0)
    for r in (1, 4, 3, 2, 0):
        send_row(1, r)
    remote(stats, stats, 0, sts.at[0], col_peer(0, 1)).wait_recv()
    group = mine[0]
    for i in range(NC - 1):
        group += stats[i]
    mine[1] = group
    for i, o in enumerate(ROW_PEERS):
        remote(mine.at[1], tot.at[i], 11, sts.at[1], row_at(*o)).start()
    from_row(4)
    for p in (0, 7, 6, 3, 5):
        send_col(1, p)
    from_row(1)
    for p in (1, 2, 4):
        send_col(1, p)

    sent(txr.at[0], 4)
    sent(txc.at[0], 5)
    sent(fcol.at[0 : NC - 1], 8)
    sent(frow.at[0 : NR - 1], 9)
    sent(stats, 10)
    further_ref[...] = total(1) + noise * first_ref[...]
    remote(tot, tot, 0, sts.at[1], col_peer(0, 1)).wait_recv()
    for i in range(len(ROW_PEERS)):
        group += tot[i]
    spread = jnp.broadcast_to(group, (NRHS, CH))
    gammas = jnp.sum(jnp.where(lane == sub, spread, 0.0), 1, keepdims=True)
    deltas = jnp.sum(jnp.where(lane == sub + NRHS, spread, 0.0), 1, keepdims=True)
    alpha_ref[...] = jnp.broadcast_to(gammas / deltas, (NRHS, CH))
    sent(txr.at[1], 6)
    sent(txc.at[1], 7)
    sent(tot, 11)


def on_device(design, lengthscales, counts, noise_base, targets):
    out = jax.ShapeDtypeStruct((NRHS, CH), F32)
    vmem, hbm = (pl.BlockSpec(memory_space=m) for m in (pltpu.VMEM, pltpu.HBM))
    dma = pltpu.SemaphoreType.DMA

    def chunks(*shape):
        return pltpu.VMEM(shape + (CH,), F32)

    alphas, first, further = pl.pallas_call(
        cg_kernel,
        out_shape=(out, out, out),
        in_specs=[hbm] * 5,
        out_specs=(vmem, vmem, vmem),
        scratch_shapes=[
            pltpu.SMEM((8,), F32), pltpu.SMEM((1,), F32), pltpu.VMEM((1, CH), jnp.int32),
            chunks(NC, 8), chunks(NR, 8), chunks(NC, NRHS), chunks(NR, NRHS), chunks(NC, NRHS), chunks(NR, NRHS),
            chunks(NC - 1, 1), chunks(len(ROW_PEERS), 1), chunks(2, 1),
            chunks(2, NR - 1, NRHS), chunks(2, NC - 1, NRHS), chunks(2, NR - 1, NRHS), chunks(2, NC - 1, NRHS),
            pltpu.VMEM((NR // 2, TILE, 64), BF16), pltpu.VMEM((NC // 2, 64, TILE), BF16),
            pltpu.VMEM((NC // 2, 2 * NRHS, TILE), BF16), pltpu.VMEM((NR // 2, 2 * NRHS, TILE), BF16),
            pltpu.VMEM((NR // 2, NC // 2, TILE, TILE), BF16), pltpu.VMEM((NR // 2, NC // 2, TILE, TILE), BF16),
            pltpu.VMEM((NR // 2, NRHS, TILE), F32), pltpu.VMEM((NC // 2, NRHS, TILE), F32),
            dma((7,)), dma((12,)), dma((NC // 2,)), dma((NR // 2,)), dma((NC // 2,)), dma((NR // 2,)),
            dma((NC // 2,)), dma((NR // 2,)), dma((2, 2)), dma((2,)),
        ],
        compiler_params=pltpu.CompilerParams(collective_id=0, has_side_effects=True),
    )(design, lengthscales, counts.reshape(1, CH), noise_base, targets)
    return alphas * targets, targets - alphas * first, first - alphas * further


def solution(mesh):
    both = ("blk", "grp")
    placed = (P(None, both), P(), P(both), P(), P(None, both))
    out = P(None, both)
    return jax.shard_map(on_device, mesh=mesh, in_specs=placed, out_specs=(out, out, out), check_vma=False)
```

```python
import functools

import jax
import jax.numpy as jnp
from jax import lax
from jax.experimental import pallas as pl
from jax.experimental.pallas import tpu as pltpu
from jax.sharding import PartitionSpec as P

MESH = pl.DeviceIdType.MESH
F32, BF16 = jnp.float32, jnp.bfloat16

NRHS = 16
CH = 128
SCALE = 2.23606797749979 * 1.4426950408889634
QUAD = 0.6931471805599453**2 / 3.0
LIN = 0.6931471805599453 / QUAD
ONE = 1.0 / QUAD
TINY = 1e-30

COLS = ((2, 2), (2, 0), (1, 2), (2, 1), (1, 1), (1, 3), (0, 0), (0, 2), (0, 1), (1, 0), (0, 3), (3, 0), (3, 3), (3, 1), (3, 2), (2, 3))
ROWS = ((0, 0), (0, 1), (4, 0), (4, 1), (1, 0), (7, 1), (2, 0), (6, 1), (3, 0), (5, 1))
NC, NR = len(COLS), len(ROWS)
OWN = COLS.index((0, 0))
TILE = 2 * CH
LAG = 3
JOBS = (
    (0, 4), (0, 3), (0, 2), (2, 2), (2, 6), (3, 4), (3, 5), (3, 3), (3, 2), (3, 6),
    (1, 0), (1, 1), (1, 2), (1, 3), (1, 4), (4, 0), (0, 0), (2, 0), (3, 0), (4, 7), (2, 7), (3, 7),
    (4, 1), (0, 1), (2, 1), (3, 1), (4, 2), (4, 6), (4, 3), (4, 4), (4, 5), (2, 3), (2, 4), (2, 5),
)
STAGES = (((0, 2, 3), (4, 5, 3, 2, 6), 10), ((1, 4), (0, 1, 7), len(JOBS)))
HALF = (0, 1, 2, 3, 4)
ONE_WAY = (0, 3)
ROW_PEERS = tuple(sorted(((dz, dc) for dz in range(8) for dc in range(2) if dz or dc), key=lambda o: -min(o[0], 8 - o[0])))


def hops(offset, sizes):
    return sum(min(d, s - d) for d, s in zip(offset, sizes))


COL_ORDER = sorted((s for s in range(NC) if s != OWN), key=lambda s: -hops(COLS[s], (4, 4)))
ROW_ORDER = sorted(range(1, NR), key=lambda s: -hops(ROWS[s], (8, 1)))


def three_parts(x):
    h = x.astype(BF16).astype(F32)
    m = (x - h).astype(BF16).astype(F32)
    return h, m, (x - h - m).astype(BF16).astype(F32)


def features(points, own):
    h, m, l = three_parts(points)
    qh, qm, ql = three_parts(jnp.sum(points * points, 0, keepdims=True))
    row = lax.broadcasted_iota(jnp.int32, points.shape, 0)
    first = 0 if own else 3
    q = jnp.where(row == first, qh, jnp.where(row == first + 1, qm, jnp.where(row == first + 2, ql, jnp.where(row < 6, 1.0, 0.0))))
    zero = jnp.zeros_like(points)
    if own:
        return jnp.concatenate([h, h, m, h, l, m, q, zero], 0)
    h, m, l = -2.0 * h, -2.0 * m, -2.0 * l
    return jnp.concatenate([h, m, h, l, h, m, q, zero], 0)


def kernel_values(d):
    d = jnp.maximum(d, TINY)
    u = d * lax.rsqrt(d)
    return (d + u * LIN + ONE) * jnp.exp2(-u)


def dot(a, b, ca, cb):
    return lax.dot_general(a, b, (((ca,), (cb,)), ((), ())), preferred_element_type=F32)


def folded(y):
    return y[:NRHS] + y[NRHS:]


def split32(v):
    h = v.astype(BF16)
    return jnp.concatenate([h, (v - h.astype(F32)).astype(BF16)], 0)


def cg_kernel(
    design_ref, scales_ref, counts_ref, noise_ref, targets_ref,
    alpha_ref, first_ref, further_ref,
    scales_sm, noise_sm, counts_vm,
    dcol, drow, tcol, trow, fcol, frow, stats, tot, mine,
    txr, txc, rxr, rxc,
    fa, fb, vc, vr, ka, kb, la, lb, yrow, ycol,
    lsem, ssem, dcr, drr, tcr, trr, fcr, frr, rxs, sts,
):
    blk, grp = lax.axis_index("blk"), lax.axis_index("grp")
    zh, core = lax.div(blk, 2), lax.rem(blk, 2)
    y, zl, x = lax.div(grp, 16), lax.rem(lax.div(grp, 4), 4), lax.rem(grp, 4)
    xs = [lax.rem(x + d, 4) for d in range(4)]
    ys = [lax.rem(y + d, 4) * 16 + zl * 4 for d in range(4)]
    zs = [lax.rem(zh * 4 + zl + d, 8) for d in range(8)]
    zblk = [lax.div(v, 4) * 2 for v in zs]
    zgrp = [lax.rem(v, 4) * 4 + y * 16 + x for v in zs]
    cores = [core, 1 - core]

    def col_at(dx, dy):
        return (blk, ys[dy % 4] + xs[dx % 4])

    def row_at(dz, dc):
        return (zblk[dz % 8] + cores[dc], zgrp[dz % 8])

    def col_peer(slot, sign):
        return col_at(sign * COLS[slot][0], sign * COLS[slot][1])

    def row_peer(slot, sign):
        return row_at(sign * ROWS[slot][0], ROWS[slot][1])

    barrier = pltpu.get_barrier_semaphore()
    for s in COL_ORDER:
        pl.semaphore_signal(barrier, inc=1, device_id=col_peer(s, 1), device_id_type=MESH)
    for o in ROW_PEERS:
        pl.semaphore_signal(barrier, inc=1, device_id=row_at(*o), device_id_type=MESH)

    local = [
        pltpu.make_async_copy(src, dst, lsem.at[i])
        for i, (src, dst) in enumerate((
            (scales_ref, scales_sm), (noise_ref, noise_sm), (counts_ref, counts_vm),
            (design_ref, dcol.at[OWN]), (design_ref, drow.at[0]), (targets_ref, tcol.at[OWN]), (targets_ref, trow.at[0]),
        ))
    ]
    for c in local:
        c.start()
    pl.semaphore_wait(barrier, len(COL_ORDER) + len(ROW_PEERS))

    def remote(src, dst, ssem_at, rsem, peer):
        return pltpu.make_async_remote_copy(
            src_ref=src, dst_ref=dst, send_sem=ssem.at[ssem_at], recv_sem=rsem, device_id=peer, device_id_type=MESH
        )

    def gather(*parts):
        order = [(hops(COLS[s], (4, 4)), 0, s) for s in COL_ORDER] + [(hops(ROWS[s], (8, 1)), 1, s) for s in ROW_ORDER]
        for _, is_row, s in sorted(order):
            for src, col, col_sem, row, row_sem, at in parts:
                if is_row:
                    remote(src, row.at[s], at + 1, row_sem.at[s // 2], row_peer(s, -1)).start()
                else:
                    remote(src, col.at[s], at, col_sem.at[s // 2], col_peer(s, -1)).start()

    def pair_wait(buf, sem, pair, own):
        lo, hi = 2 * pair, 2 * pair + 2
        lo = lo + 1 if lo == own else lo
        remote(buf.at[lo:hi], buf.at[lo:hi], 0, sem.at[pair], col_peer(0, 1)).wait_recv()

    def sent(ref, at):
        remote(ref, ref, at, rxs.at[0, 0], col_peer(0, 1)).wait_send()

    gather((design_ref, dcol, dcr, drow, drr, 0), (targets_ref, tcol, tcr, trow, trr, 2))

    for c in local:
        c.wait()
    dim = lax.broadcasted_iota(jnp.int32, (8, CH), 0)
    scales = jnp.zeros((8, CH), F32)
    for d in range(8):
        scales = jnp.where(dim == d, scales_sm[d], scales)
    noise = noise_sm[0] / counts_vm[...].astype(F32)
    yrow[...] = jnp.zeros_like(yrow)
    ycol[...] = jnp.zeros_like(ycol)

    def column_chunks(p):
        pair_wait(dcol, dcr, p, OWN)
        pair_wait(tcol, tcr, p, OWN)

    def row_chunks(r):
        pair_wait(drow, drr, r, 0)
        pair_wait(trow, trr, r, 0)

    def column_inputs(p):
        for h in (0, 1):
            fb[p, :, h * CH : (h + 1) * CH] = features(dcol[2 * p + h] / scales * SCALE, False).astype(BF16)

    def row_inputs(r):
        for h in (0, 1):
            fa[r, h * CH : (h + 1) * CH, :] = features(drow[2 * r + h] / scales * SCALE, True).T.astype(BF16)

    def vectors(buf, pair, out):
        for h in (0, 1):
            out[pair, :, h * CH : (h + 1) * CH] = split32(buf[2 * pair + h])

    place = {job: i for i, job in enumerate(JOBS)}

    def held(r, p):
        i = place[r, p]
        return (ka, kb)[i % 2].at[i // 2], (la, lb)[i % 2].at[i // 2]

    def tile(r, p):
        k = kernel_values(dot(fa[r], fb[p], 1, 0))
        high, low = held(r, p)
        hi = k.astype(BF16)
        high[...] = hi
        low[...] = (k - hi.astype(F32)).astype(BF16)

    def to_rows(r, p):
        high, low = held(r, p)
        yrow[r] += folded(dot(vc[p], high[...], 1, 1)) + dot(vc[p, 0:NRHS], low[...], 1, 1)

    def to_cols(r, p):
        if r > 1 or p not in ONE_WAY:
            high, low = held(r, p)
            ycol[p] += folded(dot(vr[r], high[...], 1, 0)) + dot(vr[r, 0:NRHS], low[...], 1, 0)

    def send_row(k, r):
        for s in (2 * r, 2 * r + 1):
            if s:
                txr[k, s - 1] = yrow[r, :, (s - 2 * r) * CH : (s - 2 * r + 1) * CH]
                remote(txr.at[k, s - 1], rxr.at[k, s - 1], 4 + 2 * k, rxs.at[k, 0], row_peer(s, 1)).start()

    def send_col(k, p):
        for s in (2 * p, 2 * p + 1):
            if s != OWN:
                i = s - (s > OWN)
                txc[k, i] = ycol[p, :, (s - 2 * p) * CH : (s - 2 * p + 1) * CH]
                remote(txc.at[k, i], rxc.at[k, i], 5 + 2 * k, rxs.at[k, 1], col_peer(s, 1)).start()

    def total(k):
        own = yrow[0, :, 0:CH] + ycol[OWN // 2, :, (OWN % 2) * CH : (OWN % 2 + 1) * CH]
        remote(rxr.at[k], rxr.at[k], 0, rxs.at[k, 0], col_peer(0, 1)).wait_recv()
        for i in range(NR - 1):
            own += rxr[k, i]
        remote(rxc.at[k], rxc.at[k], 0, rxs.at[k, 1], col_peer(0, 1)).wait_recv()
        for i in range(NC - 1):
            own += rxc[k, i]
        return own * QUAD

    rows_left = {r: sum(job[0] == r for job in JOBS) for r in range(NR // 2)}
    cols_left = {p: sum(job[1] == p for job in JOBS) for p in range(NC // 2)}
    done = 0
    for stage, (rows, cols, upto) in enumerate(STAGES):
        for r in rows:
            row_chunks(r)
        for p in cols:
            column_chunks(p)
        for r in rows:
            row_inputs(r)
            vectors(trow, r, vr)
        for p in cols:
            column_inputs(p)
            vectors(tcol, p, vc)
        last = stage == len(STAGES) - 1
        start = 0 if stage == 0 else STAGES[stage - 1][2]
        for i in range(start, upto + (LAG if last else 0)):
            if i < upto:
                tile(*JOBS[i])
            if i >= LAG:
                r, p = JOBS[i - LAG]
                to_rows(r, p)
                to_cols(r, p)
                rows_left[r] -= 1
                cols_left[p] -= 1
                if cols_left[p] == 0:
                    send_col(0, p)
                if rows_left[r] == 0:
                    send_row(0, r)

    sent(dcol.at[0 : NC - 1], 0)
    sent(drow.at[0 : NR - 1], 1)
    sent(tcol.at[0 : NC - 1], 2)
    sent(trow.at[0 : NR - 1], 3)
    own = tcol[OWN]
    lane = lax.broadcasted_iota(jnp.int32, (NRHS, CH), 1)
    sub = lax.broadcasted_iota(jnp.int32, (NRHS, CH), 0)
    gamma = jnp.sum(own * own, 1, keepdims=True)
    first = total(0) + noise * own

    fcol[OWN] = first
    frow[0] = first
    gather((fcol.at[OWN], fcol, fcr, frow, frr, 8))

    delta = jnp.sum(first * own, 1, keepdims=True)
    marked = jnp.where(lane == sub, gamma, 0.0) + jnp.where(lane == sub + NRHS, delta, 0.0)
    mine[0] = jnp.sum(marked, 0, keepdims=True)
    for s in COL_ORDER:
        remote(mine.at[0], stats.at[s - (s > OWN)], 10, sts.at[0], col_peer(s, 1)).start()
    first_ref[...] = first
    yrow[...] = jnp.zeros_like(yrow)
    ycol[...] = jnp.zeros_like(ycol)

    def second(rows, cols):
        for r in rows:
            pair_wait(frow, frr, r, 0)
        for p in cols:
            pair_wait(fcol, fcr, p, OWN)
        for r in rows:
            vectors(frow, r, vr)
        for p in cols:
            vectors(fcol, p, vc)

    def from_row(r):
        for p in HALF if r < 2 else range(8):
            to_cols(r, p)

    def from_col(p):
        for r in range(5) if p in HALF else (2, 3, 4):
            to_rows(r, p)

    second((0, 2), (4, 5))
    from_col(4)
    from_row(0)
    from_col(5)
    from_row(2)
    second((3,), (3, 2, 6))
    from_col(3)
    from_col(2)
    from_col(6)
    from_row(3)
    second((1, 4), (0, 1, 7))
    from_col(0)
    from_col(1)
    from_col(7)
    for r in (1, 4, 3, 2, 0):
        send_row(1, r)
    from_row(4)
    for p in (0, 7, 6, 3, 5):
        send_col(1, p)
    from_row(1)
    for p in (1, 2, 4):
        send_col(1, p)
    remote(stats, stats, 0, sts.at[0], col_peer(0, 1)).wait_recv()
    group = mine[0]
    for i in range(NC - 1):
        group += stats[i]
    mine[1] = group
    for i, o in enumerate(ROW_PEERS):
        remote(mine.at[1], tot.at[i], 11, sts.at[1], row_at(*o)).start()

    sent(txr.at[0], 4)
    sent(txc.at[0], 5)
    sent(fcol.at[0 : NC - 1], 8)
    sent(frow.at[0 : NR - 1], 9)
    sent(stats, 10)
    further_ref[...] = total(1) + noise * first_ref[...]
    remote(tot, tot, 0, sts.at[1], col_peer(0, 1)).wait_recv()
    for i in range(len(ROW_PEERS)):
        group += tot[i]
    spread = jnp.broadcast_to(group, (NRHS, CH))
    gammas = jnp.sum(jnp.where(lane == sub, spread, 0.0), 1, keepdims=True)
    deltas = jnp.sum(jnp.where(lane == sub + NRHS, spread, 0.0), 1, keepdims=True)
    alpha_ref[...] = jnp.broadcast_to(gammas / deltas, (NRHS, CH))
    sent(txr.at[1], 6)
    sent(txc.at[1], 7)
    sent(tot, 11)


def on_device(design, lengthscales, counts, noise_base, targets):
    out = jax.ShapeDtypeStruct((NRHS, CH), F32)
    vmem, hbm = (pl.BlockSpec(memory_space=m) for m in (pltpu.VMEM, pltpu.HBM))
    dma = pltpu.SemaphoreType.DMA

    def chunks(*shape):
        return pltpu.VMEM(shape + (CH,), F32)

    alphas, first, further = pl.pallas_call(
        cg_kernel,
        out_shape=(out, out, out),
        in_specs=[hbm] * 5,
        out_specs=(vmem, vmem, vmem),
        scratch_shapes=[
            pltpu.SMEM((8,), F32), pltpu.SMEM((1,), F32), pltpu.VMEM((1, CH), jnp.int32),
            chunks(NC, 8), chunks(NR, 8), chunks(NC, NRHS), chunks(NR, NRHS), chunks(NC, NRHS), chunks(NR, NRHS),
            chunks(NC - 1, 1), chunks(len(ROW_PEERS), 1), chunks(2, 1),
            chunks(2, NR - 1, NRHS), chunks(2, NC - 1, NRHS), chunks(2, NR - 1, NRHS), chunks(2, NC - 1, NRHS),
            pltpu.VMEM((NR // 2, TILE, 64), BF16), pltpu.VMEM((NC // 2, 64, TILE), BF16),
            pltpu.VMEM((NC // 2, 2 * NRHS, TILE), BF16), pltpu.VMEM((NR // 2, 2 * NRHS, TILE), BF16),
            *[pltpu.VMEM((len(JOBS) // 2, TILE, TILE), BF16)] * 4,
            pltpu.VMEM((NR // 2, NRHS, TILE), F32), pltpu.VMEM((NC // 2, NRHS, TILE), F32),
            dma((7,)), dma((12,)), dma((NC // 2,)), dma((NR // 2,)), dma((NC // 2,)), dma((NR // 2,)),
            dma((NC // 2,)), dma((NR // 2,)), dma((2, 2)), dma((2,)),
        ],
        compiler_params=pltpu.CompilerParams(collective_id=0, has_side_effects=True),
    )(design, lengthscales, counts.reshape(1, CH), noise_base, targets)
    return alphas * targets, targets - alphas * first, first - alphas * further


def solution(mesh):
    both = ("blk", "grp")
    placed = (P(None, both), P(), P(both), P(), P(None, both))
    out = P(None, both)
    return jax.shard_map(on_device, mesh=mesh, in_specs=placed, out_specs=(out, out, out), check_vma=False)
```

```python
import functools

import jax
import jax.numpy as jnp
from jax import lax
from jax.experimental import pallas as pl
from jax.experimental.pallas import tpu as pltpu
from jax.sharding import PartitionSpec as P

MESH = pl.DeviceIdType.MESH
F32, BF16 = jnp.float32, jnp.bfloat16

NRHS = 16
CH = 128
SCALE = 2.23606797749979 * 1.4426950408889634
QUAD = 0.6931471805599453**2 / 3.0
LIN = 0.6931471805599453 / QUAD
ONE = 1.0 / QUAD
TINY = 1e-30

COLS = ((2, 2), (2, 0), (1, 2), (2, 1), (1, 1), (1, 3), (0, 0), (0, 2), (0, 1), (1, 0), (0, 3), (3, 0), (3, 3), (3, 1), (3, 2), (2, 3))
ROWS = ((0, 0), (0, 1), (4, 0), (4, 1), (1, 0), (7, 1), (2, 0), (6, 1), (3, 0), (5, 1))
NC, NR = len(COLS), len(ROWS)
OWN = COLS.index((0, 0))
TILE = 2 * CH
BLOCKS = (
    ((0, 2, 3), (4, 5, 3, 2, 6), ((0, 4), (3, 4), (3, 5), (0, 3), (3, 3)), ()),
    ((), (), ((3, 2), (0, 2), (2, 2), (2, 6), (3, 6)), ((3, 4), (3, 5), (3, 3))),
    ((), (), ((2, 3), (2, 4), (2, 5)), ((3, 2), (0, 2), (2, 2), (2, 6), (3, 6))),
    ((1, 4), (0, 1, 7), ((1, 0), (1, 1), (1, 2), (1, 3), (1, 4)), ((2, 3),)),
    ((), (), ((4, 0), (0, 0), (2, 0), (3, 0), (4, 7)), ((1, 0), (1, 1), (1, 2), (1, 3), (1, 4))),
    ((), (), ((2, 7), (3, 7), (4, 1), (0, 1), (2, 1), (3, 1)), ((4, 0), (0, 0), (2, 0), (3, 0), (4, 7))),
    ((), (), ((4, 2), (4, 6), (4, 3), (4, 4), (4, 5)), ((2, 7), (3, 7), (4, 1), (0, 1), (2, 1), (3, 1))),
    ((), (), (), ((4, 2), (4, 6), (4, 3), (4, 4), (4, 5))),
    ((), (), (), ((0, 4), (0, 3), (2, 4), (2, 5))),
)
JOBS = tuple(job for block in BLOCKS for job in block[2])
assert len(set(JOBS)) == 34 and sorted(JOBS) == sorted(job for block in BLOCKS for job in block[3])
HALF = (0, 1, 2, 3, 4)
ONE_WAY = (0, 3)
ROW_PEERS = tuple(sorted(((dz, dc) for dz in range(8) for dc in range(2) if dz or dc), key=lambda o: -min(o[0], 8 - o[0])))


def hops(offset, sizes):
    return sum(min(d, s - d) for d, s in zip(offset, sizes))


COL_ORDER = sorted((s for s in range(NC) if s != OWN), key=lambda s: -hops(COLS[s], (4, 4)))
ROW_ORDER = sorted(range(1, NR), key=lambda s: -hops(ROWS[s], (8, 1)))


def three_parts(x):
    h = x.astype(BF16).astype(F32)
    m = (x - h).astype(BF16).astype(F32)
    return h, m, (x - h - m).astype(BF16).astype(F32)


def features(points, own):
    h, m, l = three_parts(points)
    qh, qm, ql = three_parts(jnp.sum(points * points, 0, keepdims=True))
    row = lax.broadcasted_iota(jnp.int32, points.shape, 0)
    first = 0 if own else 3
    q = jnp.where(row == first, qh, jnp.where(row == first + 1, qm, jnp.where(row == first + 2, ql, jnp.where(row < 6, 1.0, 0.0))))
    zero = jnp.zeros_like(points)
    if own:
        return jnp.concatenate([h, h, m, h, l, m, q, zero], 0)
    h, m, l = -2.0 * h, -2.0 * m, -2.0 * l
    return jnp.concatenate([h, m, h, l, h, m, q, zero], 0)


def kernel_values(d):
    d = jnp.maximum(d, TINY)
    u = d * lax.rsqrt(d)
    return (d + u * LIN + ONE) * jnp.exp2(-u)


def dot(a, b, ca, cb):
    return lax.dot_general(a, b, (((ca,), (cb,)), ((), ())), preferred_element_type=F32)


def folded(y):
    return y[:NRHS] + y[NRHS:]


def split32(v):
    h = v.astype(BF16)
    return jnp.concatenate([h, (v - h.astype(F32)).astype(BF16)], 0)


def cg_kernel(
    design_ref, scales_ref, counts_ref, noise_ref, targets_ref,
    alpha_ref, first_ref, further_ref,
    scales_sm, noise_sm, counts_vm,
    dcol, drow, tcol, trow, fcol, frow, stats, tot, mine,
    txr, txc, rxr, rxc,
    fa, fb, vc, vr, ka, kb, la, lb, yrow, ycol,
    lsem, ssem, dcr, drr, tcr, trr, fcr, frr, rxs, sts,
):
    blk, grp = lax.axis_index("blk"), lax.axis_index("grp")
    zh, core = lax.div(blk, 2), lax.rem(blk, 2)
    y, zl, x = lax.div(grp, 16), lax.rem(lax.div(grp, 4), 4), lax.rem(grp, 4)
    xs = [lax.rem(x + d, 4) for d in range(4)]
    ys = [lax.rem(y + d, 4) * 16 + zl * 4 for d in range(4)]
    zs = [lax.rem(zh * 4 + zl + d, 8) for d in range(8)]
    zblk = [lax.div(v, 4) * 2 for v in zs]
    zgrp = [lax.rem(v, 4) * 4 + y * 16 + x for v in zs]
    cores = [core, 1 - core]

    def col_at(dx, dy):
        return (blk, ys[dy % 4] + xs[dx % 4])

    def row_at(dz, dc):
        return (zblk[dz % 8] + cores[dc], zgrp[dz % 8])

    def col_peer(slot, sign):
        return col_at(sign * COLS[slot][0], sign * COLS[slot][1])

    def row_peer(slot, sign):
        return row_at(sign * ROWS[slot][0], ROWS[slot][1])

    barrier = pltpu.get_barrier_semaphore()
    peers = [(hops(COLS[s], (4, 4)), col_peer(s, 1)) for s in COL_ORDER]
    peers += [(min(o[0], 8 - o[0]), row_at(*o)) for o in ROW_PEERS]
    for _, peer in sorted(peers, key=lambda o: -o[0]):
        pl.semaphore_signal(barrier, inc=1, device_id=peer, device_id_type=MESH)

    local = [
        pltpu.make_async_copy(src, dst, lsem.at[i])
        for i, (src, dst) in enumerate((
            (scales_ref, scales_sm), (noise_ref, noise_sm), (counts_ref, counts_vm),
            (design_ref, dcol.at[OWN]), (design_ref, drow.at[0]), (targets_ref, tcol.at[OWN]), (targets_ref, trow.at[0]),
        ))
    ]
    for c in local:
        c.start()
    pl.semaphore_wait(barrier, len(COL_ORDER) + len(ROW_PEERS))

    def remote(src, dst, ssem_at, rsem, peer):
        return pltpu.make_async_remote_copy(
            src_ref=src, dst_ref=dst, send_sem=ssem.at[ssem_at], recv_sem=rsem, device_id=peer, device_id_type=MESH
        )

    def gather(*parts):
        order = [(hops(COLS[s], (4, 4)), 0, s) for s in COL_ORDER] + [(hops(ROWS[s], (8, 1)), 1, s) for s in ROW_ORDER]
        for _, is_row, s in sorted(order):
            for src, col, col_sem, row, row_sem, at in parts:
                if is_row:
                    remote(src, row.at[s], at + 1, row_sem.at[s // 2], row_peer(s, -1)).start()
                else:
                    remote(src, col.at[s], at, col_sem.at[s // 2], col_peer(s, -1)).start()

    def pair_wait(buf, sem, pair, own):
        lo, hi = 2 * pair, 2 * pair + 2
        lo = lo + 1 if lo == own else lo
        remote(buf.at[lo:hi], buf.at[lo:hi], 0, sem.at[pair], col_peer(0, 1)).wait_recv()

    def sent(ref, at):
        remote(ref, ref, at, rxs.at[0, 0], col_peer(0, 1)).wait_send()

    gather((design_ref, dcol, dcr, drow, drr, 0), (targets_ref, tcol, tcr, trow, trr, 2))

    for c in local:
        c.wait()
    dim = lax.broadcasted_iota(jnp.int32, (8, CH), 0)
    scales = jnp.zeros((8, CH), F32)
    for d in range(8):
        scales = jnp.where(dim == d, scales_sm[d], scales)
    noise = noise_sm[0] / counts_vm[...].astype(F32)
    yrow[...] = jnp.zeros_like(yrow)
    ycol[...] = jnp.zeros_like(ycol)

    def column_chunks(p):
        pair_wait(dcol, dcr, p, OWN)
        pair_wait(tcol, tcr, p, OWN)

    def row_chunks(r):
        pair_wait(drow, drr, r, 0)
        pair_wait(trow, trr, r, 0)

    def column_inputs(p):
        for h in (0, 1):
            fb[p, :, h * CH : (h + 1) * CH] = features(dcol[2 * p + h] / scales * SCALE, False).astype(BF16)

    def row_inputs(r):
        for h in (0, 1):
            fa[r, h * CH : (h + 1) * CH, :] = features(drow[2 * r + h] / scales * SCALE, True).T.astype(BF16)

    def vectors(buf, pair, out):
        for h in (0, 1):
            out[pair, :, h * CH : (h + 1) * CH] = split32(buf[2 * pair + h])

    place = {job: i for i, job in enumerate(JOBS)}

    def held(r, p):
        i = place[r, p]
        return (ka, kb)[i % 2].at[i // 2], (la, lb)[i % 2].at[i // 2]

    def tile(r, p):
        k = kernel_values(dot(fa[r], fb[p], 1, 0))
        high, low = held(r, p)
        hi = k.astype(BF16)
        high[...] = hi
        low[...] = (k - hi.astype(F32)).astype(BF16)

    def joined(values, axis):
        return jnp.concatenate(values, axis) if len(values) > 1 else values[0]

    def products(jobs):
        jobs = [(is_col, own, [o for o in over if not is_col or o > 1 or own not in ONE_WAY]) for is_col, own, over in jobs]
        jobs = [job for job in jobs if job[2]]
        operands = []
        for is_col, own, over in jobs:
            vectors_of = (vc, vr)[is_col]
            high, low = ([t[...] for t in tiles] for tiles in zip(*(held(*((o, own) if is_col else (own, o))) for o in over)))
            operands.append((joined([vectors_of[o] for o in over], 1), joined(high, 1 - is_col), joined(low, 1 - is_col)))
        first = [folded(dot(v, hi, 1, 1 - job[0])) for job, (v, hi, _) in zip(jobs, operands)]
        second = [dot(v[0:NRHS], lo, 1, 1 - job[0]) for job, (v, _, lo) in zip(jobs, operands)]
        for (is_col, own, _), a, b in zip(jobs, first, second):
            (yrow, ycol)[is_col][own] += a + b

    def apart(jobs):
        @pl.when(blk >= 0)
        def _():
            products(jobs)

    def send_row(k, r):
        for s in (2 * r, 2 * r + 1):
            if s:
                txr[k, s - 1] = yrow[r, :, (s - 2 * r) * CH : (s - 2 * r + 1) * CH]
                remote(txr.at[k, s - 1], rxr.at[k, s - 1], 4 + 2 * k, rxs.at[k, 0], row_peer(s, 1)).start()

    def send_col(k, p):
        for s in (2 * p, 2 * p + 1):
            if s != OWN:
                i = s - (s > OWN)
                txc[k, i] = ycol[p, :, (s - 2 * p) * CH : (s - 2 * p + 1) * CH]
                remote(txc.at[k, i], rxc.at[k, i], 5 + 2 * k, rxs.at[k, 1], col_peer(s, 1)).start()

    def total(k):
        own = yrow[0, :, 0:CH] + ycol[OWN // 2, :, (OWN % 2) * CH : (OWN % 2 + 1) * CH]
        remote(rxr.at[k], rxr.at[k], 0, rxs.at[k, 0], col_peer(0, 1)).wait_recv()
        for i in range(NR - 1):
            own += rxr[k, i]
        remote(rxc.at[k], rxc.at[k], 0, rxs.at[k, 1], col_peer(0, 1)).wait_recv()
        for i in range(NC - 1):
            own += rxc[k, i]
        return own * QUAD

    rows_left = {r: sum(job[0] == r for job in JOBS) for r in range(NR // 2)}
    cols_left = {p: sum(job[1] == p for job in JOBS) for p in range(NC // 2)}
    for rows, cols, values, sums in BLOCKS:
        for r in rows:
            row_chunks(r)
        for p in cols:
            column_chunks(p)

        @pl.when(blk >= 0)
        def _(rows=rows, cols=cols, values=values, sums=sums):
            for r in rows:
                row_inputs(r)
                vectors(trow, r, vr)
            for p in cols:
                column_inputs(p)
                vectors(tcol, p, vc)
            for i in range(max(len(values), len(sums))):
                if i < len(values):
                    tile(*values[i])
                if i < len(sums):
                    r, p = sums[i]
                    products([(0, r, (p,))])
                    products([(1, p, (r,))])

        for r, p in sums:
            rows_left[r] -= 1
            cols_left[p] -= 1
        for r in range(NR // 2):
            if rows_left[r] == 0:
                rows_left[r] = -1
                send_row(0, r)
        for p in range(NC // 2):
            if cols_left[p] == 0:
                cols_left[p] = -1
                send_col(0, p)

    sent(dcol.at[0 : NC - 1], 0)
    sent(drow.at[0 : NR - 1], 1)
    sent(tcol.at[0 : NC - 1], 2)
    sent(trow.at[0 : NR - 1], 3)
    own = tcol[OWN]
    lane = lax.broadcasted_iota(jnp.int32, (NRHS, CH), 1)
    sub = lax.broadcasted_iota(jnp.int32, (NRHS, CH), 0)
    gamma = jnp.sum(own * own, 1, keepdims=True)
    first = total(0) + noise * own

    fcol[OWN] = first
    frow[0] = first
    gather((fcol.at[OWN], fcol, fcr, frow, frr, 8))

    delta = jnp.sum(first * own, 1, keepdims=True)
    marked = jnp.where(lane == sub, gamma, 0.0) + jnp.where(lane == sub + NRHS, delta, 0.0)
    mine[0] = jnp.sum(marked, 0, keepdims=True)
    for s in COL_ORDER:
        remote(mine.at[0], stats.at[s - (s > OWN)], 10, sts.at[0], col_peer(s, 1)).start()
    first_ref[...] = first
    yrow[...] = jnp.zeros_like(yrow)
    ycol[...] = jnp.zeros_like(ycol)

    def second(rows, cols):
        for r in rows:
            pair_wait(frow, frr, r, 0)
        for p in cols:
            pair_wait(fcol, fcr, p, OWN)
        for r in rows:
            vectors(frow, r, vr)
        for p in cols:
            vectors(fcol, p, vc)

    near, far = ((0, 2, 3), (4, 5, 3, 2, 6)), ((1, 4), (0, 1, 7))

    def met(is_col, own, others):
        return tuple(o for o in others if ((o if is_col else own) > 1 or (own if is_col else o) in HALF))

    second(near[0], near[1])
    apart([(0, r, met(0, r, near[1])) for r in (1, 4, 3, 2, 0)])
    apart([(1, p, met(1, p, near[0])) for p in (0, 7, 1, 2, 6, 3, 4, 5)])
    second(far[0], far[1])
    apart([(0, r, met(0, r, far[1])) for r in (1, 4)])
    send_row(1, 1)
    send_row(1, 4)
    apart([(1, p, met(1, p, far[0])) for p in (0, 7, 1)] + [(0, r, met(0, r, far[1])) for r in (3, 2, 0)])
    for p in (0, 7, 1):
        send_col(1, p)
    for r in (3, 2, 0):
        send_row(1, r)
    remote(stats, stats, 0, sts.at[0], col_peer(0, 1)).wait_recv()
    group = mine[0]
    for i in range(NC - 1):
        group += stats[i]
    mine[1] = group
    for i, o in enumerate(ROW_PEERS):
        remote(mine.at[1], tot.at[i], 11, sts.at[1], row_at(*o)).start()
    apart([(1, p, met(1, p, far[0])) for p in (2, 6, 3, 4, 5)])
    for p in (2, 6, 3, 4, 5):
        send_col(1, p)

    sent(txr.at[0], 4)
    sent(txc.at[0], 5)
    sent(fcol.at[0 : NC - 1], 8)
    sent(frow.at[0 : NR - 1], 9)
    sent(stats, 10)
    further_ref[...] = total(1) + noise * first_ref[...]
    remote(tot, tot, 0, sts.at[1], col_peer(0, 1)).wait_recv()
    for i in range(len(ROW_PEERS)):
        group += tot[i]
    spread = jnp.broadcast_to(group, (NRHS, CH))
    gammas = jnp.sum(jnp.where(lane == sub, spread, 0.0), 1, keepdims=True)
    deltas = jnp.sum(jnp.where(lane == sub + NRHS, spread, 0.0), 1, keepdims=True)
    alpha_ref[...] = jnp.broadcast_to(gammas / deltas, (NRHS, CH))
    sent(txr.at[1], 6)
    sent(txc.at[1], 7)
    sent(tot, 11)


def on_device(design, lengthscales, counts, noise_base, targets):
    out = jax.ShapeDtypeStruct((NRHS, CH), F32)
    vmem, hbm = (pl.BlockSpec(memory_space=m) for m in (pltpu.VMEM, pltpu.HBM))
    dma = pltpu.SemaphoreType.DMA

    def in_hbm(a):
        return pltpu.with_memory_space_constraint(a, pltpu.HBM)

    def chunks(*shape):
        return pltpu.VMEM(shape + (CH,), F32)

    alphas, first, further = pl.pallas_call(
        cg_kernel,
        out_shape=(out, out, out),
        in_specs=[hbm] * 5,
        out_specs=(vmem, vmem, vmem),
        scratch_shapes=[
            pltpu.SMEM((8,), F32), pltpu.SMEM((1,), F32), pltpu.VMEM((1, CH), jnp.int32),
            chunks(NC, 8), chunks(NR, 8), chunks(NC, NRHS), chunks(NR, NRHS), chunks(NC, NRHS), chunks(NR, NRHS),
            chunks(NC - 1, 1), chunks(len(ROW_PEERS), 1), chunks(2, 1),
            chunks(2, NR - 1, NRHS), chunks(2, NC - 1, NRHS), chunks(2, NR - 1, NRHS), chunks(2, NC - 1, NRHS),
            pltpu.VMEM((NR // 2, TILE, 64), BF16), pltpu.VMEM((NC // 2, 64, TILE), BF16),
            pltpu.VMEM((NC // 2, 2 * NRHS, TILE), BF16), pltpu.VMEM((NR // 2, 2 * NRHS, TILE), BF16),
            *[pltpu.VMEM((len(JOBS) // 2, TILE, TILE), BF16)] * 4,
            pltpu.VMEM((NR // 2, NRHS, TILE), F32), pltpu.VMEM((NC // 2, NRHS, TILE), F32),
            dma((7,)), dma((12,)), dma((NC // 2,)), dma((NR // 2,)), dma((NC // 2,)), dma((NR // 2,)),
            dma((NC // 2,)), dma((NR // 2,)), dma((2, 2)), dma((2,)),
        ],
        compiler_params=pltpu.CompilerParams(collective_id=0, has_side_effects=True, vmem_limit_bytes=48 << 20),
    )(in_hbm(design), in_hbm(lengthscales), in_hbm(counts.reshape(1, CH)), noise_base, in_hbm(targets))
    return alphas * targets, targets - alphas * first, first - alphas * further


def solution(mesh):
    both = ("blk", "grp")
    placed = (P(None, both), P(), P(both), P(), P(None, both))
    out = P(None, both)
    return jax.shard_map(on_device, mesh=mesh, in_specs=placed, out_specs=(out, out, out), check_vma=False)
```

```python
import functools

import jax
import jax.numpy as jnp
from jax import lax
from jax.experimental import pallas as pl
from jax.experimental.pallas import tpu as pltpu
from jax.sharding import PartitionSpec as P

MESH = pl.DeviceIdType.MESH
F32, BF16 = jnp.float32, jnp.bfloat16

NRHS = 16
CH = 128
SCALE = 2.23606797749979 * 1.4426950408889634
QUAD = 0.6931471805599453**2 / 3.0
LIN = 0.6931471805599453 / QUAD
ONE = 1.0 / QUAD
TINY = 1e-30

COLS = ((2, 2), (2, 0), (1, 2), (2, 1), (1, 1), (1, 3), (0, 0), (0, 2), (0, 1), (1, 0), (0, 3), (3, 0), (3, 3), (3, 1), (3, 2), (2, 3))
ROWS = ((0, 0), (0, 1), (4, 0), (4, 1), (1, 0), (7, 1), (2, 0), (6, 1), (3, 0), (5, 1))
NC, NR = len(COLS), len(ROWS)
OWN = COLS.index((0, 0))
TILE = 2 * CH
NEAR, FAR, NONE = ((0, 2, 3), (4, 5, 3, 2, 6)), ((1, 4), (0, 1, 7)), ((), ())
BLOCKS = (
    (NEAR, NONE, ((3, 4), (3, 5), (3, 3), (3, 2), (0, 2)), ()),
    (NONE, NEAR, ((2, 2), (2, 6), (3, 6), (0, 4), (0, 3)), ((3, 4), (3, 5), (3, 3), (3, 2), (0, 2))),
    (FAR, NONE, ((1, 0), (1, 1), (1, 2), (1, 3), (1, 4)), ((2, 2), (2, 6), (3, 6))),
    (NONE, FAR, ((4, 0), (0, 0), (2, 0), (3, 0), (4, 7), (2, 7)), ((1, 0), (1, 1), (1, 2), (1, 3), (1, 4))),
    (NONE, NONE, ((3, 7), (4, 1), (0, 1), (2, 1), (3, 1)), ((4, 0), (0, 0), (2, 0), (3, 0), (4, 7), (2, 7))),
    (NONE, NONE, ((4, 2), (4, 6), (4, 3), (4, 4), (4, 5)), ((3, 7), (4, 1), (0, 1), (2, 1), (3, 1))),
    (NONE, NONE, ((2, 3), (2, 4), (2, 5)), ((4, 2), (4, 6), (4, 3), (4, 4), (4, 5))),
    (NONE, NONE, (), ((0, 4), (0, 3), (2, 3), (2, 4), (2, 5))),
)
JOBS = tuple(job for block in BLOCKS for job in block[2])
assert len(set(JOBS)) == 34 and sorted(JOBS) == sorted(job for block in BLOCKS for job in block[3])
HALF = (0, 1, 2, 3, 4)
ONE_WAY = (0, 3)
ROW_PEERS = tuple(sorted(((dz, dc) for dz in range(8) for dc in range(2) if dz or dc), key=lambda o: -min(o[0], 8 - o[0])))


def hops(offset, sizes):
    return sum(min(d, s - d) for d, s in zip(offset, sizes))


COL_ORDER = sorted((s for s in range(NC) if s != OWN), key=lambda s: -hops(COLS[s], (4, 4)))
ROW_ORDER = sorted(range(1, NR), key=lambda s: -hops(ROWS[s], (8, 1)))


def three_parts(x):
    h = x.astype(BF16).astype(F32)
    m = (x - h).astype(BF16).astype(F32)
    return h, m, (x - h - m).astype(BF16).astype(F32)


def features(points, own):
    h, m, l = three_parts(points)
    qh, qm, ql = three_parts(jnp.sum(points * points, 0, keepdims=True))
    row = lax.broadcasted_iota(jnp.int32, points.shape, 0)
    first = 0 if own else 3
    q = jnp.where(row == first, qh, jnp.where(row == first + 1, qm, jnp.where(row == first + 2, ql, jnp.where(row < 6, 1.0, 0.0))))
    zero = jnp.zeros_like(points)
    if own:
        return jnp.concatenate([h, h, m, h, l, m, q, zero], 0)
    h, m, l = -2.0 * h, -2.0 * m, -2.0 * l
    return jnp.concatenate([h, m, h, l, h, m, q, zero], 0)


def kernel_values(d):
    d = jnp.maximum(d, TINY)
    u = d * lax.rsqrt(d)
    return (d + u * LIN + ONE) * jnp.exp2(-u)


def dot(a, b, ca, cb):
    return lax.dot_general(a, b, (((ca,), (cb,)), ((), ())), preferred_element_type=F32)


def folded(y):
    return y[:NRHS] + y[NRHS:]


def split32(v):
    h = v.astype(BF16)
    return jnp.concatenate([h, (v - h.astype(F32)).astype(BF16)], 0)


def cg_kernel(
    design_ref, scales_ref, counts_ref, noise_ref, targets_ref,
    alpha_ref, first_ref, further_ref,
    scales_sm, noise_sm, counts_vm,
    dcol, drow, tcol, trow, fcol, frow, stats, tot, mine,
    txr, txc, rxr, rxc,
    fa, fb, vc, vr, ka, kb, la, lb, yrow, ycol,
    lsem, ssem, dcr, drr, tcr, trr, fcr, frr, rxs, sts,
):
    blk, grp = lax.axis_index("blk"), lax.axis_index("grp")
    zh, core = lax.div(blk, 2), lax.rem(blk, 2)
    y, zl, x = lax.div(grp, 16), lax.rem(lax.div(grp, 4), 4), lax.rem(grp, 4)
    xs = [lax.rem(x + d, 4) for d in range(4)]
    ys = [lax.rem(y + d, 4) * 16 + zl * 4 for d in range(4)]
    zs = [lax.rem(zh * 4 + zl + d, 8) for d in range(8)]
    zblk = [lax.div(v, 4) * 2 for v in zs]
    zgrp = [lax.rem(v, 4) * 4 + y * 16 + x for v in zs]
    cores = [core, 1 - core]

    def col_at(dx, dy):
        return (blk, ys[dy % 4] + xs[dx % 4])

    def row_at(dz, dc):
        return (zblk[dz % 8] + cores[dc], zgrp[dz % 8])

    def col_peer(slot, sign):
        return col_at(sign * COLS[slot][0], sign * COLS[slot][1])

    def row_peer(slot, sign):
        return row_at(sign * ROWS[slot][0], ROWS[slot][1])

    barrier = pltpu.get_barrier_semaphore()
    peers = [(hops(COLS[s], (4, 4)), col_peer(s, 1)) for s in COL_ORDER]
    peers += [(min(o[0], 8 - o[0]), row_at(*o)) for o in ROW_PEERS]
    for _, peer in sorted(peers, key=lambda o: -o[0]):
        pl.semaphore_signal(barrier, inc=1, device_id=peer, device_id_type=MESH)

    local = [
        pltpu.make_async_copy(src, dst, lsem.at[i])
        for i, (src, dst) in enumerate((
            (scales_ref, scales_sm), (noise_ref, noise_sm), (counts_ref, counts_vm),
            (design_ref, dcol.at[OWN]), (design_ref, drow.at[0]), (targets_ref, tcol.at[OWN]), (targets_ref, trow.at[0]),
        ))
    ]
    for c in local:
        c.start()
    pl.semaphore_wait(barrier, len(COL_ORDER) + len(ROW_PEERS))

    def remote(src, dst, ssem_at, rsem, peer):
        return pltpu.make_async_remote_copy(
            src_ref=src, dst_ref=dst, send_sem=ssem.at[ssem_at], recv_sem=rsem, device_id=peer, device_id_type=MESH
        )

    def gather(*parts):
        order = [(hops(COLS[s], (4, 4)), 0, s) for s in COL_ORDER] + [(hops(ROWS[s], (8, 1)), 1, s) for s in ROW_ORDER]
        for _, is_row, s in sorted(order):
            for src, col, col_sem, row, row_sem, at in parts:
                if is_row:
                    remote(src, row.at[s], at + 1, row_sem.at[s // 2], row_peer(s, -1)).start()
                else:
                    remote(src, col.at[s], at, col_sem.at[s // 2], col_peer(s, -1)).start()

    def pair_wait(buf, sem, pair, own):
        lo, hi = 2 * pair, 2 * pair + 2
        lo = lo + 1 if lo == own else lo
        remote(buf.at[lo:hi], buf.at[lo:hi], 0, sem.at[pair], col_peer(0, 1)).wait_recv()

    def sent(ref, at):
        remote(ref, ref, at, rxs.at[0, 0], col_peer(0, 1)).wait_send()

    gather((design_ref, dcol, dcr, drow, drr, 0))
    gather((targets_ref, tcol, tcr, trow, trr, 2))

    for c in local:
        c.wait()
    dim = lax.broadcasted_iota(jnp.int32, (8, CH), 0)
    scales = jnp.zeros((8, CH), F32)
    for d in range(8):
        scales = jnp.where(dim == d, scales_sm[d], scales)
    noise = noise_sm[0] / counts_vm[...].astype(F32)
    yrow[...] = jnp.zeros_like(yrow)
    ycol[...] = jnp.zeros_like(ycol)

    def column_inputs(p):
        for h in (0, 1):
            fb[p, :, h * CH : (h + 1) * CH] = features(dcol[2 * p + h] / scales * SCALE, False).astype(BF16)

    def row_inputs(r):
        for h in (0, 1):
            fa[r, h * CH : (h + 1) * CH, :] = features(drow[2 * r + h] / scales * SCALE, True).T.astype(BF16)

    def vectors(buf, pair, out):
        for h in (0, 1):
            out[pair, :, h * CH : (h + 1) * CH] = split32(buf[2 * pair + h])

    place = {job: i for i, job in enumerate(JOBS)}

    def held(r, p):
        i = place[r, p]
        return (ka, kb)[i % 2].at[i // 2], (la, lb)[i % 2].at[i // 2]

    def tile(r, p):
        k = kernel_values(dot(fa[r], fb[p], 1, 0))
        high, low = held(r, p)
        hi = k.astype(BF16)
        high[...] = hi
        low[...] = (k - hi.astype(F32)).astype(BF16)

    def joined(values, axis):
        return jnp.concatenate(values, axis) if len(values) > 1 else values[0]

    def products(jobs):
        jobs = [(is_col, own, [o for o in over if not is_col or o > 1 or own not in ONE_WAY]) for is_col, own, over in jobs]
        jobs = [job for job in jobs if job[2]]
        operands = []
        for is_col, own, over in jobs:
            vectors_of = (vc, vr)[is_col]
            high, low = ([t[...] for t in tiles] for tiles in zip(*(held(*((o, own) if is_col else (own, o))) for o in over)))
            operands.append((joined([vectors_of[o] for o in over], 1), joined(high, 1 - is_col), joined(low, 1 - is_col)))
        first = [folded(dot(v, hi, 1, 1 - job[0])) for job, (v, hi, _) in zip(jobs, operands)]
        second = [dot(v[0:NRHS], lo, 1, 1 - job[0]) for job, (v, _, lo) in zip(jobs, operands)]
        for (is_col, own, _), a, b in zip(jobs, first, second):
            (yrow, ycol)[is_col][own] += a + b

    def apart(jobs):
        @pl.when(blk >= 0)
        def _():
            products(jobs)

    def send_row(k, r):
        for s in (2 * r, 2 * r + 1):
            if s:
                txr[k, s - 1] = yrow[r, :, (s - 2 * r) * CH : (s - 2 * r + 1) * CH]
                remote(txr.at[k, s - 1], rxr.at[k, s - 1], 4 + 2 * k, rxs.at[k, 0], row_peer(s, 1)).start()

    def send_col(k, p):
        for s in (2 * p, 2 * p + 1):
            if s != OWN:
                i = s - (s > OWN)
                txc[k, i] = ycol[p, :, (s - 2 * p) * CH : (s - 2 * p + 1) * CH]
                remote(txc.at[k, i], rxc.at[k, i], 5 + 2 * k, rxs.at[k, 1], col_peer(s, 1)).start()

    def total(k):
        own = yrow[0, :, 0:CH] + ycol[OWN // 2, :, (OWN % 2) * CH : (OWN % 2 + 1) * CH]
        remote(rxr.at[k], rxr.at[k], 0, rxs.at[k, 0], col_peer(0, 1)).wait_recv()
        for i in range(NR - 1):
            own += rxr[k, i]
        remote(rxc.at[k], rxc.at[k], 0, rxs.at[k, 1], col_peer(0, 1)).wait_recv()
        for i in range(NC - 1):
            own += rxc[k, i]
        return own * QUAD

    rows_left = {r: sum(job[0] == r for job in JOBS) for r in range(NR // 2)}
    cols_left = {p: sum(job[1] == p for job in JOBS) for p in range(NC // 2)}
    for points, targets, values, sums in BLOCKS:
        for r in points[0]:
            pair_wait(drow, drr, r, 0)
        for p in points[1]:
            pair_wait(dcol, dcr, p, OWN)
        for r in targets[0]:
            pair_wait(trow, trr, r, 0)
        for p in targets[1]:
            pair_wait(tcol, tcr, p, OWN)

        @pl.when(blk >= 0)
        def _(points=points, targets=targets, values=values, sums=sums):
            for r in points[0]:
                row_inputs(r)
            for p in points[1]:
                column_inputs(p)
            for r in targets[0]:
                vectors(trow, r, vr)
            for p in targets[1]:
                vectors(tcol, p, vc)
            for i in range(max(len(values), len(sums))):
                if i < len(values):
                    tile(*values[i])
                if i < len(sums):
                    r, p = sums[i]
                    products([(0, r, (p,))])
                    products([(1, p, (r,))])

        for r, p in sums:
            rows_left[r] -= 1
            cols_left[p] -= 1
        for r in range(NR // 2):
            if rows_left[r] == 0:
                rows_left[r] = -1
                send_row(0, r)
        for p in range(NC // 2):
            if cols_left[p] == 0:
                cols_left[p] = -1
                send_col(0, p)

    sent(dcol.at[0 : NC - 1], 0)
    sent(drow.at[0 : NR - 1], 1)
    sent(tcol.at[0 : NC - 1], 2)
    sent(trow.at[0 : NR - 1], 3)
    own = tcol[OWN]
    lane = lax.broadcasted_iota(jnp.int32, (NRHS, CH), 1)
    sub = lax.broadcasted_iota(jnp.int32, (NRHS, CH), 0)
    gamma = jnp.sum(own * own, 1, keepdims=True)
    first = total(0) + noise * own

    fcol[OWN] = first
    frow[0] = first
    gather((fcol.at[OWN], fcol, fcr, frow, frr, 8))

    delta = jnp.sum(first * own, 1, keepdims=True)
    marked = jnp.where(lane == sub, gamma, 0.0) + jnp.where(lane == sub + NRHS, delta, 0.0)
    mine[0] = jnp.sum(marked, 0, keepdims=True)
    for s in COL_ORDER:
        remote(mine.at[0], stats.at[s - (s > OWN)], 10, sts.at[0], col_peer(s, 1)).start()
    first_ref[...] = first
    yrow[...] = jnp.zeros_like(yrow)
    ycol[...] = jnp.zeros_like(ycol)

    def second(rows, cols):
        for r in rows:
            pair_wait(frow, frr, r, 0)
        for p in cols:
            pair_wait(fcol, fcr, p, OWN)
        for r in rows:
            vectors(frow, r, vr)
        for p in cols:
            vectors(fcol, p, vc)

    def met(is_col, own, others):
        return tuple(o for o in others if ((o if is_col else own) > 1 or (own if is_col else o) in HALF))

    second(NEAR[0], NEAR[1])
    apart([(0, r, met(0, r, NEAR[1])) for r in (1, 4)] + [(1, p, met(1, p, NEAR[0])) for p in (0, 7, 1)])
    second(FAR[0], FAR[1])
    apart([(0, r, met(0, r, FAR[1])) for r in (1, 4)])
    send_row(1, 1)
    send_row(1, 4)
    apart([(1, p, met(1, p, FAR[0])) for p in (0, 7, 1)])
    for p in (0, 7, 1):
        send_col(1, p)
    remote(stats, stats, 0, sts.at[0], col_peer(0, 1)).wait_recv()
    group = mine[0]
    for i in range(NC - 1):
        group += stats[i]
    mine[1] = group
    for i, o in enumerate(ROW_PEERS):
        remote(mine.at[1], tot.at[i], 11, sts.at[1], row_at(*o)).start()
    apart([(0, r, met(0, r, range(NC // 2))) for r in (3, 2)])
    send_row(1, 3)
    send_row(1, 2)
    apart([(1, p, met(1, p, range(NR // 2))) for p in (2, 6, 3, 4, 5)] + [(0, 0, HALF)])
    for p in (2, 6, 3, 4, 5):
        send_col(1, p)
    send_row(1, 0)

    sent(txr.at[0], 4)
    sent(txc.at[0], 5)
    sent(fcol.at[0 : NC - 1], 8)
    sent(frow.at[0 : NR - 1], 9)
    sent(stats, 10)
    further_ref[...] = total(1) + noise * first_ref[...]
    remote(tot, tot, 0, sts.at[1], col_peer(0, 1)).wait_recv()
    for i in range(len(ROW_PEERS)):
        group += tot[i]
    spread = jnp.broadcast_to(group, (NRHS, CH))
    gammas = jnp.sum(jnp.where(lane == sub, spread, 0.0), 1, keepdims=True)
    deltas = jnp.sum(jnp.where(lane == sub + NRHS, spread, 0.0), 1, keepdims=True)
    alpha_ref[...] = jnp.broadcast_to(gammas / deltas, (NRHS, CH))
    sent(txr.at[1], 6)
    sent(txc.at[1], 7)
    sent(tot, 11)


def on_device(design, lengthscales, counts, noise_base, targets):
    out = jax.ShapeDtypeStruct((NRHS, CH), F32)
    vmem, hbm = (pl.BlockSpec(memory_space=m) for m in (pltpu.VMEM, pltpu.HBM))
    dma = pltpu.SemaphoreType.DMA

    def in_hbm(a):
        return pltpu.with_memory_space_constraint(a, pltpu.HBM)

    def chunks(*shape):
        return pltpu.VMEM(shape + (CH,), F32)

    alphas, first, further = pl.pallas_call(
        cg_kernel,
        out_shape=(out, out, out),
        in_specs=[hbm] * 5,
        out_specs=(vmem, vmem, vmem),
        scratch_shapes=[
            pltpu.SMEM((8,), F32), pltpu.SMEM((1,), F32), pltpu.VMEM((1, CH), jnp.int32),
            chunks(NC, 8), chunks(NR, 8), chunks(NC, NRHS), chunks(NR, NRHS), chunks(NC, NRHS), chunks(NR, NRHS),
            chunks(NC - 1, 1), chunks(len(ROW_PEERS), 1), chunks(2, 1),
            chunks(2, NR - 1, NRHS), chunks(2, NC - 1, NRHS), chunks(2, NR - 1, NRHS), chunks(2, NC - 1, NRHS),
            pltpu.VMEM((NR // 2, TILE, 64), BF16), pltpu.VMEM((NC // 2, 64, TILE), BF16),
            pltpu.VMEM((NC // 2, 2 * NRHS, TILE), BF16), pltpu.VMEM((NR // 2, 2 * NRHS, TILE), BF16),
            *[pltpu.VMEM((len(JOBS) // 2, TILE, TILE), BF16)] * 4,
            pltpu.VMEM((NR // 2, NRHS, TILE), F32), pltpu.VMEM((NC // 2, NRHS, TILE), F32),
            dma((7,)), dma((12,)), dma((NC // 2,)), dma((NR // 2,)), dma((NC // 2,)), dma((NR // 2,)),
            dma((NC // 2,)), dma((NR // 2,)), dma((2, 2)), dma((2,)),
        ],
        compiler_params=pltpu.CompilerParams(collective_id=0, has_side_effects=True, vmem_limit_bytes=48 << 20),
    )(in_hbm(design), in_hbm(lengthscales), in_hbm(counts.reshape(1, CH)), noise_base, in_hbm(targets))
    return alphas * targets, targets - alphas * first, first - alphas * further


def solution(mesh):
    both = ("blk", "grp")
    placed = (P(None, both), P(), P(both), P(), P(None, both))
    out = P(None, both)
    return jax.shard_map(on_device, mesh=mesh, in_specs=placed, out_specs=(out, out, out), check_vma=False)
```

```python
import functools

import jax
import jax.numpy as jnp
from jax import lax
from jax.experimental import pallas as pl
from jax.experimental.pallas import tpu as pltpu
from jax.sharding import PartitionSpec as P

MESH = pl.DeviceIdType.MESH
F32, BF16 = jnp.float32, jnp.bfloat16

NRHS = 16
CH = 128
SCALE = 2.23606797749979 * 1.4426950408889634
QUAD = 0.6931471805599453**2 / 3.0
LIN = 0.6931471805599453 / QUAD
ONE = 1.0 / QUAD
TINY = 1e-30

COLS = ((2, 2), (2, 0), (1, 2), (2, 1), (1, 1), (1, 3), (0, 0), (0, 2), (0, 1), (1, 0), (0, 3), (3, 0), (3, 3), (3, 1), (3, 2), (2, 3))
ROWS = ((0, 0), (0, 1), (4, 0), (4, 1), (1, 0), (7, 1), (2, 0), (6, 1), (3, 0), (5, 1))
NC, NR = len(COLS), len(ROWS)
OWN = COLS.index((0, 0))
TILE = 2 * CH
NEAR, FAR, NONE = ((0, 2, 3), (4, 5, 3, 2, 6)), ((1, 4), (0, 1, 7)), ((), ())
BLOCKS = (
    (NEAR, NONE, ((3, 4), (3, 5), (3, 3), (3, 2), (0, 2)), ()),
    (NONE, NEAR, ((2, 2), (2, 6), (3, 6), (0, 4), (0, 3)), ((3, 4), (3, 5), (3, 3), (3, 2), (0, 2))),
    (FAR, NONE, ((1, 0), (1, 1), (1, 2), (1, 3), (1, 4)), ((2, 2), (2, 6), (3, 6))),
    (NONE, FAR, ((4, 0), (0, 0), (2, 0), (3, 0), (4, 7), (2, 7)), ((1, 0), (1, 1), (1, 2), (1, 3), (1, 4))),
    (NONE, NONE, ((3, 7), (4, 1), (0, 1), (2, 1), (3, 1)), ((4, 0), (0, 0), (2, 0), (3, 0), (4, 7), (2, 7))),
    (NONE, NONE, ((4, 2), (4, 6), (4, 3), (4, 4), (4, 5)), ((3, 7), (4, 1), (0, 1), (2, 1), (3, 1))),
    (NONE, NONE, ((2, 3), (2, 4), (2, 5)), ((4, 2), (4, 6), (4, 3), (4, 4), (4, 5))),
    (NONE, NONE, (), ((0, 4), (0, 3), (2, 3), (2, 4), (2, 5))),
)
JOBS = tuple(job for block in BLOCKS for job in block[2])
assert len(set(JOBS)) == 34 and sorted(JOBS) == sorted(job for block in BLOCKS for job in block[3])
HALF = (0, 1, 2, 3, 4)
ONE_WAY = (0, 3)
ROW_PEERS = tuple(sorted(((dz, dc) for dz in range(8) for dc in range(2) if dz or dc), key=lambda o: -min(o[0], 8 - o[0])))


def hops(offset, sizes):
    return sum(min(d, s - d) for d, s in zip(offset, sizes))


COL_ORDER = sorted((s for s in range(NC) if s != OWN), key=lambda s: -hops(COLS[s], (4, 4)))
ROW_ORDER = sorted(range(1, NR), key=lambda s: -hops(ROWS[s], (8, 1)))


def three_parts(x):
    h = x.astype(BF16).astype(F32)
    m = (x - h).astype(BF16).astype(F32)
    return h, m, (x - h - m).astype(BF16).astype(F32)


def features(points, own):
    h, m, l = three_parts(points)
    qh, qm, ql = three_parts(jnp.sum(points * points, 0, keepdims=True))
    row = lax.broadcasted_iota(jnp.int32, points.shape, 0)
    first = 0 if own else 3
    q = jnp.where(row == first, qh, jnp.where(row == first + 1, qm, jnp.where(row == first + 2, ql, jnp.where(row < 6, 1.0, 0.0))))
    zero = jnp.zeros_like(points)
    if own:
        return jnp.concatenate([h, h, m, h, l, m, q, zero], 0)
    h, m, l = -2.0 * h, -2.0 * m, -2.0 * l
    return jnp.concatenate([h, m, h, l, h, m, q, zero], 0)


def kernel_values(d):
    d = jnp.maximum(d, TINY)
    u = d * lax.rsqrt(d)
    return (d + u * LIN + ONE) * jnp.exp2(-u)


def dot(a, b, ca, cb):
    return lax.dot_general(a, b, (((ca,), (cb,)), ((), ())), preferred_element_type=F32)


def folded(y):
    return y[:NRHS] + y[NRHS:]


def split32(v):
    h = v.astype(BF16)
    return jnp.concatenate([h, (v - h.astype(F32)).astype(BF16)], 0)


def cg_kernel(
    design_ref, scales_ref, counts_ref, noise_ref, targets_ref,
    alpha_ref, first_ref, further_ref,
    scales_sm, noise_sm, counts_vm,
    dcol, drow, tcol, trow, fcol, frow, stats, tot, mine,
    txr, txc, rxr, rxc,
    fa, fb, vc, vr, ka, kb, la, lb, kt, lt, yrow, ycol,
    lsem, ssem, dcr, drr, tcr, trr, fcr, frr, rxs, sts,
):
    blk, grp = lax.axis_index("blk"), lax.axis_index("grp")
    zh, core = lax.div(blk, 2), lax.rem(blk, 2)
    y, zl, x = lax.div(grp, 16), lax.rem(lax.div(grp, 4), 4), lax.rem(grp, 4)
    xs = [lax.rem(x + d, 4) for d in range(4)]
    ys = [lax.rem(y + d, 4) * 16 + zl * 4 for d in range(4)]
    zs = [lax.rem(zh * 4 + zl + d, 8) for d in range(8)]
    zblk = [lax.div(v, 4) * 2 for v in zs]
    zgrp = [lax.rem(v, 4) * 4 + y * 16 + x for v in zs]
    cores = [core, 1 - core]

    def col_at(dx, dy):
        return (blk, ys[dy % 4] + xs[dx % 4])

    def row_at(dz, dc):
        return (zblk[dz % 8] + cores[dc], zgrp[dz % 8])

    def col_peer(slot, sign):
        return col_at(sign * COLS[slot][0], sign * COLS[slot][1])

    def row_peer(slot, sign):
        return row_at(sign * ROWS[slot][0], ROWS[slot][1])

    barrier = pltpu.get_barrier_semaphore()
    peers = [(hops(COLS[s], (4, 4)), col_peer(s, 1)) for s in COL_ORDER]
    peers += [(min(o[0], 8 - o[0]), row_at(*o)) for o in ROW_PEERS]
    for _, peer in sorted(peers, key=lambda o: -o[0]):
        pl.semaphore_signal(barrier, inc=1, device_id=peer, device_id_type=MESH)

    local = [
        pltpu.make_async_copy(src, dst, lsem.at[i])
        for i, (src, dst) in enumerate((
            (scales_ref, scales_sm), (noise_ref, noise_sm), (counts_ref, counts_vm),
            (design_ref, dcol.at[OWN]), (design_ref, drow.at[0]), (targets_ref, tcol.at[OWN]), (targets_ref, trow.at[0]),
        ))
    ]
    for c in local:
        c.start()
    pl.semaphore_wait(barrier, len(COL_ORDER) + len(ROW_PEERS))

    def remote(src, dst, ssem_at, rsem, peer):
        return pltpu.make_async_remote_copy(
            src_ref=src, dst_ref=dst, send_sem=ssem.at[ssem_at], recv_sem=rsem, device_id=peer, device_id_type=MESH
        )

    def gather(*parts):
        order = [(hops(COLS[s], (4, 4)), 0, s) for s in COL_ORDER] + [(hops(ROWS[s], (8, 1)), 1, s) for s in ROW_ORDER]
        for _, is_row, s in sorted(order):
            for src, col, col_sem, row, row_sem, at in parts:
                if is_row:
                    remote(src, row.at[s], at + 1, row_sem.at[s // 2], row_peer(s, -1)).start()
                else:
                    remote(src, col.at[s], at, col_sem.at[s // 2], col_peer(s, -1)).start()

    def pair_wait(buf, sem, pair, own):
        lo, hi = 2 * pair, 2 * pair + 2
        lo = lo + 1 if lo == own else lo
        remote(buf.at[lo:hi], buf.at[lo:hi], 0, sem.at[pair], col_peer(0, 1)).wait_recv()

    def sent(ref, at):
        remote(ref, ref, at, rxs.at[0, 0], col_peer(0, 1)).wait_send()

    gather((design_ref, dcol, dcr, drow, drr, 0))
    gather((targets_ref, tcol, tcr, trow, trr, 2))

    for c in local:
        c.wait()
    dim = lax.broadcasted_iota(jnp.int32, (8, CH), 0)
    scales = jnp.zeros((8, CH), F32)
    for d in range(8):
        scales = jnp.where(dim == d, scales_sm[d], scales)
    noise = noise_sm[0] / counts_vm[...].astype(F32)
    yrow[...] = jnp.zeros_like(yrow)
    ycol[...] = jnp.zeros_like(ycol)

    def column_inputs(p):
        for h in (0, 1):
            fb[p, :, h * CH : (h + 1) * CH] = features(dcol[2 * p + h] / scales * SCALE, False).astype(BF16)

    def row_inputs(r):
        for h in (0, 1):
            fa[r, h * CH : (h + 1) * CH, :] = features(drow[2 * r + h] / scales * SCALE, True).T.astype(BF16)

    def vectors(buf, pair, out):
        for h in (0, 1):
            out[pair, :, h * CH : (h + 1) * CH] = split32(buf[2 * pair + h])

    place = {job: i for i, job in enumerate(JOBS)}

    def held(r, p):
        i = place[r, p]
        return (ka, kb)[i % 2].at[i // 2], (la, lb)[i % 2].at[i // 2]

    def tile(r, p):
        k = kernel_values(dot(fa[r], fb[p], 1, 0))
        high, low = held(r, p)
        hi = k.astype(BF16)
        high[...] = hi
        low[...] = (k - hi.astype(F32)).astype(BF16)

    def joined(values, axis):
        return jnp.concatenate(values, axis) if len(values) > 1 else values[0]

    def turn(jobs):
        @pl.when(blk >= 0)
        def _():
            for job in jobs:
                for of, to in zip(held(*job), (kt, lt)):
                    to[place[job]] = of[...].T

    def products(jobs, turned=False):
        jobs = [(is_col, own, [o for o in over if not is_col or o > 1 or own not in ONE_WAY]) for is_col, own, over in jobs]
        jobs = [job for job in jobs if job[2]]
        operands = []
        for is_col, own, over in jobs:
            vectors_of = (vc, vr)[is_col]
            at = 0 if is_col or turned else 1
            if turned and not is_col:
                high, low = ([t[place[own, o]] for o in over] for t in (kt, lt))
            else:
                high, low = ([t[...] for t in tiles] for tiles in zip(*(held(*((o, own) if is_col else (own, o))) for o in over)))
            operands.append((joined([vectors_of[o] for o in over], 1), joined(high, at), joined(low, at), at))
        first = [folded(dot(v, hi, 1, at)) for v, hi, _, at in operands]
        second = [dot(v[0:NRHS], lo, 1, at) for v, _, lo, at in operands]
        for (is_col, own, _), a, b in zip(jobs, first, second):
            (yrow, ycol)[is_col][own] += a + b

    def apart(jobs):
        @pl.when(blk >= 0)
        def _():
            products(jobs, True)

    def send_row(k, r):
        for s in (2 * r, 2 * r + 1):
            if s:
                txr[k, s - 1] = yrow[r, :, (s - 2 * r) * CH : (s - 2 * r + 1) * CH]
                remote(txr.at[k, s - 1], rxr.at[k, s - 1], 4 + 2 * k, rxs.at[k, 0], row_peer(s, 1)).start()

    def send_col(k, p):
        for s in (2 * p, 2 * p + 1):
            if s != OWN:
                i = s - (s > OWN)
                txc[k, i] = ycol[p, :, (s - 2 * p) * CH : (s - 2 * p + 1) * CH]
                remote(txc.at[k, i], rxc.at[k, i], 5 + 2 * k, rxs.at[k, 1], col_peer(s, 1)).start()

    def total(k):
        own = yrow[0, :, 0:CH] + ycol[OWN // 2, :, (OWN % 2) * CH : (OWN % 2 + 1) * CH]
        remote(rxr.at[k], rxr.at[k], 0, rxs.at[k, 0], col_peer(0, 1)).wait_recv()
        for i in range(NR - 1):
            own += rxr[k, i]
        remote(rxc.at[k], rxc.at[k], 0, rxs.at[k, 1], col_peer(0, 1)).wait_recv()
        for i in range(NC - 1):
            own += rxc[k, i]
        return own * QUAD

    rows_left = {r: sum(job[0] == r for job in JOBS) for r in range(NR // 2)}
    cols_left = {p: sum(job[1] == p for job in JOBS) for p in range(NC // 2)}
    for points, targets, values, sums in BLOCKS:
        for r in points[0]:
            pair_wait(drow, drr, r, 0)
        for p in points[1]:
            pair_wait(dcol, dcr, p, OWN)
        for r in targets[0]:
            pair_wait(trow, trr, r, 0)
        for p in targets[1]:
            pair_wait(tcol, tcr, p, OWN)

        @pl.when(blk >= 0)
        def _(points=points, targets=targets, values=values, sums=sums):
            for r in points[0]:
                row_inputs(r)
            for p in points[1]:
                column_inputs(p)
            for r in targets[0]:
                vectors(trow, r, vr)
            for p in targets[1]:
                vectors(tcol, p, vc)
            for i in range(max(len(values), len(sums))):
                if i < len(values):
                    tile(*values[i])
                if i < len(sums):
                    r, p = sums[i]
                    products([(0, r, (p,))])
                    products([(1, p, (r,))])

        for r, p in sums:
            rows_left[r] -= 1
            cols_left[p] -= 1
        for r in range(NR // 2):
            if rows_left[r] == 0:
                rows_left[r] = -1
                send_row(0, r)
        for p in range(NC // 2):
            if cols_left[p] == 0:
                cols_left[p] = -1
                send_col(0, p)

    turn(JOBS[0:20])
    sent(dcol.at[0 : NC - 1], 0)
    sent(drow.at[0 : NR - 1], 1)
    sent(tcol.at[0 : NC - 1], 2)
    sent(trow.at[0 : NR - 1], 3)
    own = tcol[OWN]
    lane = lax.broadcasted_iota(jnp.int32, (NRHS, CH), 1)
    sub = lax.broadcasted_iota(jnp.int32, (NRHS, CH), 0)
    gamma = jnp.sum(own * own, 1, keepdims=True)
    first = total(0) + noise * own

    fcol[OWN] = first
    frow[0] = first
    gather((fcol.at[OWN], fcol, fcr, frow, frr, 8))

    delta = jnp.sum(first * own, 1, keepdims=True)
    marked = jnp.where(lane == sub, gamma, 0.0) + jnp.where(lane == sub + NRHS, delta, 0.0)
    mine[0] = jnp.sum(marked, 0, keepdims=True)
    for s in COL_ORDER:
        remote(mine.at[0], stats.at[s - (s > OWN)], 10, sts.at[0], col_peer(s, 1)).start()
    first_ref[...] = first
    yrow[...] = jnp.zeros_like(yrow)
    ycol[...] = jnp.zeros_like(ycol)

    turn(JOBS[20:])

    def second(rows, cols):
        for r in rows:
            pair_wait(frow, frr, r, 0)
        for p in cols:
            pair_wait(fcol, fcr, p, OWN)
        for r in rows:
            vectors(frow, r, vr)
        for p in cols:
            vectors(fcol, p, vc)

    def met(is_col, own, others):
        return tuple(o for o in others if ((o if is_col else own) > 1 or (own if is_col else o) in HALF))

    second(NEAR[0], NEAR[1])
    apart([(0, r, met(0, r, NEAR[1])) for r in (1, 4)] + [(1, p, met(1, p, NEAR[0])) for p in (0, 7, 1)])
    second(FAR[0], FAR[1])
    apart([(0, r, met(0, r, FAR[1])) for r in (1, 4)])
    send_row(1, 1)
    send_row(1, 4)
    apart([(1, p, met(1, p, FAR[0])) for p in (0, 7, 1)])
    for p in (0, 7, 1):
        send_col(1, p)
    remote(stats, stats, 0, sts.at[0], col_peer(0, 1)).wait_recv()
    group = mine[0]
    for i in range(NC - 1):
        group += stats[i]
    mine[1] = group
    for i, o in enumerate(ROW_PEERS):
        remote(mine.at[1], tot.at[i], 11, sts.at[1], row_at(*o)).start()
    apart([(0, r, met(0, r, range(NC // 2))) for r in (3, 2)])
    send_row(1, 3)
    send_row(1, 2)
    apart([(1, p, met(1, p, range(NR // 2))) for p in (2, 6, 3, 4, 5)] + [(0, 0, HALF)])
    for p in (2, 6, 3, 4, 5):
        send_col(1, p)
    send_row(1, 0)

    sent(txr.at[0], 4)
    sent(txc.at[0], 5)
    sent(fcol.at[0 : NC - 1], 8)
    sent(frow.at[0 : NR - 1], 9)
    sent(stats, 10)
    further_ref[...] = total(1) + noise * first_ref[...]
    remote(tot, tot, 0, sts.at[1], col_peer(0, 1)).wait_recv()
    for i in range(len(ROW_PEERS)):
        group += tot[i]
    spread = jnp.broadcast_to(group, (NRHS, CH))
    gammas = jnp.sum(jnp.where(lane == sub, spread, 0.0), 1, keepdims=True)
    deltas = jnp.sum(jnp.where(lane == sub + NRHS, spread, 0.0), 1, keepdims=True)
    alpha_ref[...] = jnp.broadcast_to(gammas / deltas, (NRHS, CH))
    sent(txr.at[1], 6)
    sent(txc.at[1], 7)
    sent(tot, 11)


def on_device(design, lengthscales, counts, noise_base, targets):
    out = jax.ShapeDtypeStruct((NRHS, CH), F32)
    vmem, hbm = (pl.BlockSpec(memory_space=m) for m in (pltpu.VMEM, pltpu.HBM))
    dma = pltpu.SemaphoreType.DMA

    def in_hbm(a):
        return pltpu.with_memory_space_constraint(a, pltpu.HBM)

    def chunks(*shape):
        return pltpu.VMEM(shape + (CH,), F32)

    alphas, first, further = pl.pallas_call(
        cg_kernel,
        out_shape=(out, out, out),
        in_specs=[hbm] * 5,
        out_specs=(vmem, vmem, vmem),
        scratch_shapes=[
            pltpu.SMEM((8,), F32), pltpu.SMEM((1,), F32), pltpu.VMEM((1, CH), jnp.int32),
            chunks(NC, 8), chunks(NR, 8), chunks(NC, NRHS), chunks(NR, NRHS), chunks(NC, NRHS), chunks(NR, NRHS),
            chunks(NC - 1, 1), chunks(len(ROW_PEERS), 1), chunks(2, 1),
            chunks(2, NR - 1, NRHS), chunks(2, NC - 1, NRHS), chunks(2, NR - 1, NRHS), chunks(2, NC - 1, NRHS),
            pltpu.VMEM((NR // 2, TILE, 64), BF16), pltpu.VMEM((NC // 2, 64, TILE), BF16),
            pltpu.VMEM((NC // 2, 2 * NRHS, TILE), BF16), pltpu.VMEM((NR // 2, 2 * NRHS, TILE), BF16),
            *[pltpu.VMEM((len(JOBS) // 2, TILE, TILE), BF16)] * 4, *[pltpu.VMEM((len(JOBS), TILE, TILE), BF16)] * 2,
            pltpu.VMEM((NR // 2, NRHS, TILE), F32), pltpu.VMEM((NC // 2, NRHS, TILE), F32),
            dma((7,)), dma((12,)), dma((NC // 2,)), dma((NR // 2,)), dma((NC // 2,)), dma((NR // 2,)),
            dma((NC // 2,)), dma((NR // 2,)), dma((2, 2)), dma((2,)),
        ],
        compiler_params=pltpu.CompilerParams(collective_id=0, has_side_effects=True, vmem_limit_bytes=48 << 20),
    )(in_hbm(design), in_hbm(lengthscales), in_hbm(counts.reshape(1, CH)), noise_base, in_hbm(targets))
    return alphas * targets, targets - alphas * first, first - alphas * further


def solution(mesh):
    both = ("blk", "grp")
    placed = (P(None, both), P(), P(both), P(), P(None, both))
    out = P(None, both)
    return jax.shard_map(on_device, mesh=mesh, in_specs=placed, out_specs=(out, out, out), check_vma=False)
```

```python
import functools

import jax
import jax.numpy as jnp
from jax import lax
from jax.experimental import pallas as pl
from jax.experimental.pallas import tpu as pltpu
from jax.sharding import PartitionSpec as P

MESH = pl.DeviceIdType.MESH
F32, BF16 = jnp.float32, jnp.bfloat16

NRHS = 16
CH = 128
SCALE = 2.23606797749979 * 1.4426950408889634
QUAD = 0.6931471805599453**2 / 3.0
LIN = 0.6931471805599453 / QUAD
ONE = 1.0 / QUAD
TINY = 1e-30

COLS = ((2, 2), (2, 0), (1, 2), (2, 1), (1, 1), (1, 3), (0, 0), (0, 2), (0, 1), (1, 0), (0, 3), (3, 0), (3, 3), (3, 1), (3, 2), (2, 3))
ROWS = ((0, 0), (0, 1), (4, 0), (4, 1), (1, 0), (7, 1), (2, 0), (6, 1), (3, 0), (5, 1))
NC, NR = len(COLS), len(ROWS)
OWN = COLS.index((0, 0))
TILE = 2 * CH
NEAR, FAR, NONE = ((0, 2, 3), (4, 5, 3, 2, 6)), ((1, 4), (0, 1, 7)), ((), ())
BLOCKS = (
    (NEAR, NONE, ((3, 4), (3, 5), (3, 3), (3, 2), (0, 2)), ()),
    (NONE, NEAR, ((2, 2), (2, 6), (3, 6), (0, 4), (0, 3)), ((3, 4), (3, 5), (3, 3), (3, 2), (0, 2))),
    (FAR, NONE, ((1, 0), (1, 1), (1, 2), (1, 3), (1, 4)), ((2, 2), (2, 6), (3, 6))),
    (NONE, FAR, ((4, 0), (0, 0), (2, 0), (3, 0), (4, 7), (2, 7)), ((1, 0), (1, 1), (1, 2), (1, 3), (1, 4))),
    (NONE, NONE, ((3, 7), (4, 1), (0, 1), (2, 1), (3, 1)), ((4, 0), (0, 0), (2, 0), (3, 0), (4, 7), (2, 7))),
    (NONE, NONE, ((4, 2), (4, 6), (4, 3), (4, 4), (4, 5)), ((3, 7), (4, 1), (0, 1), (2, 1), (3, 1))),
    (NONE, NONE, ((2, 3), (2, 4), (2, 5)), ((4, 2), (4, 6), (4, 3), (4, 4), (4, 5))),
    (NONE, NONE, (), ((0, 4), (0, 3), (2, 3), (2, 4), (2, 5))),
)
JOBS = tuple(job for block in BLOCKS for job in block[2])
assert len(set(JOBS)) == 34 and sorted(JOBS) == sorted(job for block in BLOCKS for job in block[3])
HALF = (0, 1, 2, 3, 4)
ONE_WAY = (0, 3)
ROW_PEERS = tuple(sorted(((dz, dc) for dz in range(8) for dc in range(2) if dz or dc), key=lambda o: -min(o[0], 8 - o[0])))


def hops(offset, sizes):
    return sum(min(d, s - d) for d, s in zip(offset, sizes))


COL_ORDER = sorted((s for s in range(NC) if s != OWN), key=lambda s: -hops(COLS[s], (4, 4)))
ROW_ORDER = sorted(range(1, NR), key=lambda s: -hops(ROWS[s], (8, 1)))


def three_parts(x):
    h = x.astype(BF16).astype(F32)
    m = (x - h).astype(BF16).astype(F32)
    return h, m, (x - h - m).astype(BF16).astype(F32)


def features(points, own):
    h, m, l = three_parts(points)
    qh, qm, ql = three_parts(jnp.sum(points * points, 0, keepdims=True))
    row = lax.broadcasted_iota(jnp.int32, points.shape, 0)
    first = 0 if own else 3
    q = jnp.where(row == first, qh, jnp.where(row == first + 1, qm, jnp.where(row == first + 2, ql, jnp.where(row < 6, 1.0, 0.0))))
    zero = jnp.zeros_like(points)
    if own:
        return jnp.concatenate([h, h, m, h, l, m, q, zero], 0)
    h, m, l = -2.0 * h, -2.0 * m, -2.0 * l
    return jnp.concatenate([h, m, h, l, h, m, q, zero], 0)


def kernel_values(d):
    d = jnp.maximum(d, TINY)
    u = d * lax.rsqrt(d)
    return (d + u * LIN + ONE) * jnp.exp2(-u)


def dot(a, b, ca, cb):
    return lax.dot_general(a, b, (((ca,), (cb,)), ((), ())), preferred_element_type=F32)


def folded(y):
    return y[:NRHS] + y[NRHS:]


def split32(v):
    h = v.astype(BF16)
    return jnp.concatenate([h, (v - h.astype(F32)).astype(BF16)], 0)


def cg_kernel(
    design_ref, scales_ref, counts_ref, noise_ref, targets_ref,
    alpha_ref, first_ref, further_ref,
    scales_sm, noise_sm, counts_vm,
    dcol, drow, tcol, trow, fcol, frow, stats, tot, mine,
    txr, txc, rxr, rxc,
    fa, fb, vc, vr, ka, kb, la, lb, kt, lt, yrow, ycol,
    lsem, ssem, dcr, drr, tcr, trr, fcr, frr, rxs, sts,
):
    blk, grp = lax.axis_index("blk"), lax.axis_index("grp")
    zh, core = lax.div(blk, 2), lax.rem(blk, 2)
    y, zl, x = lax.div(grp, 16), lax.rem(lax.div(grp, 4), 4), lax.rem(grp, 4)
    xs = [lax.rem(x + d, 4) for d in range(4)]
    ys = [lax.rem(y + d, 4) * 16 + zl * 4 for d in range(4)]
    zs = [lax.rem(zh * 4 + zl + d, 8) for d in range(8)]
    zblk = [lax.div(v, 4) * 2 for v in zs]
    zgrp = [lax.rem(v, 4) * 4 + y * 16 + x for v in zs]
    cores = [core, 1 - core]

    def col_at(dx, dy):
        return (blk, ys[dy % 4] + xs[dx % 4])

    def row_at(dz, dc):
        return (zblk[dz % 8] + cores[dc], zgrp[dz % 8])

    def col_peer(slot, sign):
        return col_at(sign * COLS[slot][0], sign * COLS[slot][1])

    def row_peer(slot, sign):
        return row_at(sign * ROWS[slot][0], ROWS[slot][1])

    barrier = pltpu.get_barrier_semaphore()
    peers = [(hops(COLS[s], (4, 4)), col_peer(s, 1)) for s in COL_ORDER]
    peers += [(min(o[0], 8 - o[0]), row_at(*o)) for o in ROW_PEERS]
    for _, peer in sorted(peers, key=lambda o: -o[0]):
        pl.semaphore_signal(barrier, inc=1, device_id=peer, device_id_type=MESH)

    local = [
        pltpu.make_async_copy(src, dst, lsem.at[i])
        for i, (src, dst) in enumerate((
            (scales_ref, scales_sm), (noise_ref, noise_sm), (counts_ref, counts_vm),
            (design_ref, dcol.at[OWN]), (design_ref, drow.at[0]), (targets_ref, tcol.at[OWN]), (targets_ref, trow.at[0]),
        ))
    ]
    for c in local:
        c.start()
    pl.semaphore_wait(barrier, len(COL_ORDER) + len(ROW_PEERS))

    def remote(src, dst, ssem_at, rsem, peer):
        return pltpu.make_async_remote_copy(
            src_ref=src, dst_ref=dst, send_sem=ssem.at[ssem_at], recv_sem=rsem, device_id=peer, device_id_type=MESH
        )

    def gather(*parts):
        order = [(hops(COLS[s], (4, 4)), 0, s) for s in COL_ORDER] + [(hops(ROWS[s], (8, 1)), 1, s) for s in ROW_ORDER]
        for _, is_row, s in sorted(order):
            for src, col, col_sem, row, row_sem, at in parts:
                if is_row:
                    remote(src, row.at[s], at + 1, row_sem.at[s // 2], row_peer(s, -1)).start()
                else:
                    remote(src, col.at[s], at, col_sem.at[s // 2], col_peer(s, -1)).start()

    def pair_wait(buf, sem, pair, own):
        lo, hi = 2 * pair, 2 * pair + 2
        lo = lo + 1 if lo == own else lo
        remote(buf.at[lo:hi], buf.at[lo:hi], 0, sem.at[pair], col_peer(0, 1)).wait_recv()

    def sent(ref, at):
        remote(ref, ref, at, rxs.at[0, 0], col_peer(0, 1)).wait_send()

    gather((design_ref, dcol, dcr, drow, drr, 0))
    gather((targets_ref, tcol, tcr, trow, trr, 2))

    for c in local:
        c.wait()
    dim = lax.broadcasted_iota(jnp.int32, (8, CH), 0)
    scales = jnp.zeros((8, CH), F32)
    for d in range(8):
        scales = jnp.where(dim == d, scales_sm[d], scales)
    noise = noise_sm[0] / counts_vm[...].astype(F32)
    yrow[...] = jnp.zeros_like(yrow)
    ycol[...] = jnp.zeros_like(ycol)

    def column_inputs(p):
        for h in (0, 1):
            fb[p, :, h * CH : (h + 1) * CH] = features(dcol[2 * p + h] / scales * SCALE, False).astype(BF16)

    def row_inputs(r):
        for h in (0, 1):
            fa[r, h * CH : (h + 1) * CH, :] = features(drow[2 * r + h] / scales * SCALE, True).T.astype(BF16)

    def vectors(buf, pair, out):
        for h in (0, 1):
            out[pair, :, h * CH : (h + 1) * CH] = split32(buf[2 * pair + h])

    place = {job: i for i, job in enumerate(JOBS)}

    def held(r, p):
        i = place[r, p]
        return (ka, kb)[i % 2].at[i // 2], (la, lb)[i % 2].at[i // 2]

    def tile(r, p):
        k = kernel_values(dot(fa[r], fb[p], 1, 0))
        high, low = held(r, p)
        hi = k.astype(BF16)
        high[...] = hi
        low[...] = (k - hi.astype(F32)).astype(BF16)

    def joined(values, axis):
        return jnp.concatenate(values, axis) if len(values) > 1 else values[0]

    def turn(jobs):
        @pl.when(blk >= 0)
        def _():
            for job in jobs:
                for of, to in zip(held(*job), (kt, lt)):
                    to[place[job]] = of[...].T

    def products(jobs, turned=False):
        jobs = [(is_col, own, [o for o in over if not is_col or o > 1 or own not in ONE_WAY]) for is_col, own, over in jobs]
        jobs = [job for job in jobs if job[2]]
        operands = []
        for is_col, own, over in jobs:
            vectors_of = (vc, vr)[is_col]
            at = 0 if is_col or turned else 1
            if turned and not is_col:
                high, low = ([t[place[own, o]] for o in over] for t in (kt, lt))
            else:
                high, low = ([t[...] for t in tiles] for tiles in zip(*(held(*((o, own) if is_col else (own, o))) for o in over)))
            operands.append((joined([vectors_of[o] for o in over], 1), joined(high, at), joined(low, at), at))
        first = [folded(dot(v, hi, 1, at)) for v, hi, _, at in operands]
        second = [dot(v[0:NRHS], lo, 1, at) for v, _, lo, at in operands]
        for (is_col, own, _), a, b in zip(jobs, first, second):
            (yrow, ycol)[is_col][own] += a + b

    def apart(jobs):
        @pl.when(blk >= 0)
        def _():
            products(jobs, True)

    def send_row(k, r):
        for s in (2 * r, 2 * r + 1):
            if s:
                txr[k, s - 1] = yrow[r, :, (s - 2 * r) * CH : (s - 2 * r + 1) * CH]
                remote(txr.at[k, s - 1], rxr.at[k, s - 1], 4 + 2 * k, rxs.at[k, 0], row_peer(s, 1)).start()

    def send_col(k, p):
        for s in (2 * p, 2 * p + 1):
            if s != OWN:
                i = s - (s > OWN)
                txc[k, i] = ycol[p, :, (s - 2 * p) * CH : (s - 2 * p + 1) * CH]
                remote(txc.at[k, i], rxc.at[k, i], 5 + 2 * k, rxs.at[k, 1], col_peer(s, 1)).start()

    def total(k):
        own = yrow[0, :, 0:CH] + ycol[OWN // 2, :, (OWN % 2) * CH : (OWN % 2 + 1) * CH]
        remote(rxr.at[k], rxr.at[k], 0, rxs.at[k, 0], col_peer(0, 1)).wait_recv()
        for i in range(NR - 1):
            own += rxr[k, i]
        remote(rxc.at[k], rxc.at[k], 0, rxs.at[k, 1], col_peer(0, 1)).wait_recv()
        for i in range(NC - 1):
            own += rxc[k, i]
        return own * QUAD

    rows_left = {r: sum(job[0] == r for job in JOBS) for r in range(NR // 2)}
    cols_left = {p: sum(job[1] == p for job in JOBS) for p in range(NC // 2)}
    for points, targets, values, sums in BLOCKS:
        for r in points[0]:
            pair_wait(drow, drr, r, 0)
        for p in points[1]:
            pair_wait(dcol, dcr, p, OWN)
        for r in targets[0]:
            pair_wait(trow, trr, r, 0)
        for p in targets[1]:
            pair_wait(tcol, tcr, p, OWN)

        @pl.when(blk >= 0)
        def _(points=points, targets=targets, values=values, sums=sums):
            for r in points[0]:
                row_inputs(r)
            for p in points[1]:
                column_inputs(p)
            for r in targets[0]:
                vectors(trow, r, vr)
            for p in targets[1]:
                vectors(tcol, p, vc)
            if not values:
                rows_of = {r: [q for t, q in sums if t == r] for r, _ in sums}
                cols_of = {p: [t for t, q in sums if q == p] for _, p in sums}
                products([(0, r, ps) for r, ps in rows_of.items()] + [(1, p, rs) for p, rs in cols_of.items()])
                return
            for i in range(max(len(values), len(sums))):
                if i < len(values):
                    tile(*values[i])
                if i < len(sums):
                    r, p = sums[i]
                    products([(0, r, (p,))])
                    products([(1, p, (r,))])

        for r, p in sums:
            rows_left[r] -= 1
            cols_left[p] -= 1
        for r in range(NR // 2):
            if rows_left[r] == 0:
                rows_left[r] = -1
                send_row(0, r)
        for p in range(NC // 2):
            if cols_left[p] == 0:
                cols_left[p] = -1
                send_col(0, p)

    turn(JOBS[0:20])
    sent(dcol.at[0 : NC - 1], 0)
    sent(drow.at[0 : NR - 1], 1)
    sent(tcol.at[0 : NC - 1], 2)
    sent(trow.at[0 : NR - 1], 3)
    own = tcol[OWN]
    lane = lax.broadcasted_iota(jnp.int32, (NRHS, CH), 1)
    sub = lax.broadcasted_iota(jnp.int32, (NRHS, CH), 0)
    gamma = jnp.sum(own * own, 1, keepdims=True)
    first = total(0) + noise * own

    fcol[OWN] = first
    frow[0] = first
    gather((fcol.at[OWN], fcol, fcr, frow, frr, 8))

    delta = jnp.sum(first * own, 1, keepdims=True)
    marked = jnp.where(lane == sub, gamma, 0.0) + jnp.where(lane == sub + NRHS, delta, 0.0)
    mine[0] = jnp.sum(marked, 0, keepdims=True)
    for s in COL_ORDER:
        remote(mine.at[0], stats.at[s - (s > OWN)], 10, sts.at[0], col_peer(s, 1)).start()
    first_ref[...] = first
    yrow[...] = jnp.zeros_like(yrow)
    ycol[...] = jnp.zeros_like(ycol)

    turn(JOBS[20:])

    def second(rows, cols):
        for r in rows:
            pair_wait(frow, frr, r, 0)
        for p in cols:
            pair_wait(fcol, fcr, p, OWN)
        for r in rows:
            vectors(frow, r, vr)
        for p in cols:
            vectors(fcol, p, vc)

    def met(is_col, own, others):
        return tuple(o for o in others if ((o if is_col else own) > 1 or (own if is_col else o) in HALF))

    second((), NEAR[1])
    apart([(0, r, met(0, r, NEAR[1])) for r in (1, 4, 3, 2)])
    second(NEAR[0], ())
    apart([(1, p, met(1, p, NEAR[0])) for p in (0, 7, 1)])
    second((), FAR[1])
    apart([(0, r, met(0, r, FAR[1])) for r in (1, 4)])
    send_row(1, 1)
    send_row(1, 4)
    second(FAR[0], ())
    apart([(1, p, met(1, p, FAR[0])) for p in (0, 7, 1)])
    for p in (0, 7, 1):
        send_col(1, p)
    remote(stats, stats, 0, sts.at[0], col_peer(0, 1)).wait_recv()
    group = mine[0]
    for i in range(NC - 1):
        group += stats[i]
    mine[1] = group
    for i, o in enumerate(ROW_PEERS):
        remote(mine.at[1], tot.at[i], 11, sts.at[1], row_at(*o)).start()
    apart([(0, r, met(0, r, FAR[1])) for r in (3, 2)])
    send_row(1, 3)
    send_row(1, 2)
    apart([(1, p, met(1, p, range(NR // 2))) for p in (2, 6, 3, 4, 5)] + [(0, 0, HALF)])
    for p in (2, 6, 3, 4, 5):
        send_col(1, p)
    send_row(1, 0)

    sent(txr.at[0], 4)
    sent(txc.at[0], 5)
    sent(fcol.at[0 : NC - 1], 8)
    sent(frow.at[0 : NR - 1], 9)
    sent(stats, 10)
    further_ref[...] = total(1) + noise * first_ref[...]
    remote(tot, tot, 0, sts.at[1], col_peer(0, 1)).wait_recv()
    for i in range(len(ROW_PEERS)):
        group += tot[i]
    spread = jnp.broadcast_to(group, (NRHS, CH))
    gammas = jnp.sum(jnp.where(lane == sub, spread, 0.0), 1, keepdims=True)
    deltas = jnp.sum(jnp.where(lane == sub + NRHS, spread, 0.0), 1, keepdims=True)
    alpha_ref[...] = jnp.broadcast_to(gammas / deltas, (NRHS, CH))
    sent(txr.at[1], 6)
    sent(txc.at[1], 7)
    sent(tot, 11)


def on_device(design, lengthscales, counts, noise_base, targets):
    out = jax.ShapeDtypeStruct((NRHS, CH), F32)
    vmem, hbm = (pl.BlockSpec(memory_space=m) for m in (pltpu.VMEM, pltpu.HBM))
    dma = pltpu.SemaphoreType.DMA

    def in_hbm(a):
        return pltpu.with_memory_space_constraint(a, pltpu.HBM)

    def chunks(*shape):
        return pltpu.VMEM(shape + (CH,), F32)

    alphas, first, further = pl.pallas_call(
        cg_kernel,
        out_shape=(out, out, out),
        in_specs=[hbm] * 5,
        out_specs=(vmem, vmem, vmem),
        scratch_shapes=[
            pltpu.SMEM((8,), F32), pltpu.SMEM((1,), F32), pltpu.VMEM((1, CH), jnp.int32),
            chunks(NC, 8), chunks(NR, 8), chunks(NC, NRHS), chunks(NR, NRHS), chunks(NC, NRHS), chunks(NR, NRHS),
            chunks(NC - 1, 1), chunks(len(ROW_PEERS), 1), chunks(2, 1),
            chunks(2, NR - 1, NRHS), chunks(2, NC - 1, NRHS), chunks(2, NR - 1, NRHS), chunks(2, NC - 1, NRHS),
            pltpu.VMEM((NR // 2, TILE, 64), BF16), pltpu.VMEM((NC // 2, 64, TILE), BF16),
            pltpu.VMEM((NC // 2, 2 * NRHS, TILE), BF16), pltpu.VMEM((NR // 2, 2 * NRHS, TILE), BF16),
            *[pltpu.VMEM((len(JOBS) // 2, TILE, TILE), BF16)] * 4, *[pltpu.VMEM((len(JOBS), TILE, TILE), BF16)] * 2,
            pltpu.VMEM((NR // 2, NRHS, TILE), F32), pltpu.VMEM((NC // 2, NRHS, TILE), F32),
            dma((7,)), dma((12,)), dma((NC // 2,)), dma((NR // 2,)), dma((NC // 2,)), dma((NR // 2,)),
            dma((NC // 2,)), dma((NR // 2,)), dma((2, 2)), dma((2,)),
        ],
        compiler_params=pltpu.CompilerParams(collective_id=0, has_side_effects=True, vmem_limit_bytes=48 << 20),
    )(in_hbm(design), in_hbm(lengthscales), in_hbm(counts.reshape(1, CH)), noise_base, in_hbm(targets))
    return alphas * targets, targets - alphas * first, first - alphas * further


def solution(mesh):
    both = ("blk", "grp")
    placed = (P(None, both), P(), P(both), P(), P(None, both))
    out = P(None, both)
    return jax.shard_map(on_device, mesh=mesh, in_specs=placed, out_specs=(out, out, out), check_vma=False)
```

```python
import functools

import jax
import jax.numpy as jnp
from jax import lax
from jax.experimental import pallas as pl
from jax.experimental.pallas import tpu as pltpu
from jax.sharding import PartitionSpec as P

MESH = pl.DeviceIdType.MESH
F32, BF16 = jnp.float32, jnp.bfloat16

NRHS = 16
CH = 128
SCALE = 2.23606797749979 * 1.4426950408889634
QUAD = 0.6931471805599453**2 / 3.0
LIN = 0.6931471805599453 / QUAD
ONE = 1.0 / QUAD
TINY = 1e-30

COLS = ((2, 2), (2, 0), (1, 2), (2, 1), (1, 1), (1, 3), (0, 0), (0, 2), (0, 1), (1, 0), (0, 3), (3, 0), (3, 3), (3, 1), (3, 2), (2, 3))
ROWS = ((0, 0), (0, 1), (4, 0), (4, 1), (1, 0), (7, 1), (2, 0), (6, 1), (3, 0), (5, 1))
NC, NR = len(COLS), len(ROWS)
OWN = COLS.index((0, 0))
TILE = 2 * CH
NEAR, FAR, NONE = ((0, 2, 3), (4, 5, 3, 2, 6)), ((1, 4), (0, 1, 7)), ((), ())
BLOCKS = (
    (NEAR, NONE, ((3, 4), (3, 5), (3, 3), (3, 2), (0, 2)), ()),
    (NONE, NEAR, ((2, 2), (2, 6), (3, 6), (0, 4), (0, 3)), ((3, 4), (3, 5), (3, 3), (3, 2), (0, 2))),
    (FAR, NONE, ((1, 0), (1, 1), (1, 2), (1, 3), (1, 4)), ((2, 2), (2, 6), (3, 6))),
    (NONE, FAR, ((4, 0), (0, 0), (2, 0), (3, 0), (4, 7), (2, 7)), ((1, 0), (1, 1), (1, 2), (1, 3), (1, 4))),
    (NONE, NONE, ((3, 7), (4, 1), (0, 1), (2, 1), (3, 1)), ((4, 0), (0, 0), (2, 0), (3, 0), (4, 7), (2, 7))),
    (NONE, NONE, ((4, 2), (4, 6), (4, 3), (4, 4), (4, 5)), ((3, 7), (4, 1), (0, 1), (2, 1), (3, 1))),
    (NONE, NONE, ((2, 3), (2, 4), (2, 5)), ((4, 2), (4, 6), (4, 3), (4, 4), (4, 5))),
    (NONE, NONE, (), ((0, 4), (0, 3), (2, 3), (2, 4), (2, 5))),
)
JOBS = tuple(job for block in BLOCKS for job in block[2])
assert len(set(JOBS)) == 34 and sorted(JOBS) == sorted(job for block in BLOCKS for job in block[3])
HALF = (0, 1, 2, 3, 4)
ONE_WAY = (0, 3)
ROW_PEERS = tuple(sorted(((dz, dc) for dz in range(8) for dc in range(2) if dz or dc), key=lambda o: -min(o[0], 8 - o[0])))


def hops(offset, sizes):
    return sum(min(d, s - d) for d, s in zip(offset, sizes))


COL_ORDER = sorted((s for s in range(NC) if s != OWN), key=lambda s: -hops(COLS[s], (4, 4)))
ROW_ORDER = sorted(range(1, NR), key=lambda s: -hops(ROWS[s], (8, 1)))


def three_parts(x):
    h = x.astype(BF16).astype(F32)
    m = (x - h).astype(BF16).astype(F32)
    return h, m, (x - h - m).astype(BF16).astype(F32)


def features(points, own):
    h, m, l = three_parts(points)
    qh, qm, ql = three_parts(jnp.sum(points * points, 0, keepdims=True))
    row = lax.broadcasted_iota(jnp.int32, points.shape, 0)
    first = 0 if own else 3
    q = jnp.where(row == first, qh, jnp.where(row == first + 1, qm, jnp.where(row == first + 2, ql, jnp.where(row < 6, 1.0, 0.0))))
    zero = jnp.zeros_like(points)
    if own:
        return jnp.concatenate([h, h, m, h, l, m, q, zero], 0)
    h, m, l = -2.0 * h, -2.0 * m, -2.0 * l
    return jnp.concatenate([h, m, h, l, h, m, q, zero], 0)


def kernel_values(d):
    d = jnp.maximum(d, TINY)
    u = d * lax.rsqrt(d)
    return (d + u * LIN + ONE) * jnp.exp2(-u)


def dot(a, b, ca, cb):
    return lax.dot_general(a, b, (((ca,), (cb,)), ((), ())), preferred_element_type=F32)


def folded(y):
    return y[:NRHS] + y[NRHS:]


def split32(v):
    h = v.astype(BF16)
    return jnp.concatenate([h, (v - h.astype(F32)).astype(BF16)], 0)


def cg_kernel(
    design_ref, scales_ref, counts_ref, noise_ref, targets_ref,
    alpha_ref, first_ref, further_ref,
    scales_sm, noise_sm, counts_vm,
    dcol, drow, tcol, trow, fcol, frow, stats, tot, mine,
    txr, txc, rxr, rxc,
    fa, fb, vc, vr, ka, kb, la, lb, kt, lt, yrow, ycol,
    lsem, ssem, dcr, drr, tcr, trr, fcr, frr, rxs, sts,
):
    blk, grp = lax.axis_index("blk"), lax.axis_index("grp")
    zh, core = lax.div(blk, 2), lax.rem(blk, 2)
    y, zl, x = lax.div(grp, 16), lax.rem(lax.div(grp, 4), 4), lax.rem(grp, 4)
    xs = [lax.rem(x + d, 4) for d in range(4)]
    ys = [lax.rem(y + d, 4) * 16 + zl * 4 for d in range(4)]
    zs = [lax.rem(zh * 4 + zl + d, 8) for d in range(8)]
    zblk = [lax.div(v, 4) * 2 for v in zs]
    zgrp = [lax.rem(v, 4) * 4 + y * 16 + x for v in zs]
    cores = [core, 1 - core]

    def col_at(dx, dy):
        return (blk, ys[dy % 4] + xs[dx % 4])

    def row_at(dz, dc):
        return (zblk[dz % 8] + cores[dc], zgrp[dz % 8])

    def col_peer(slot, sign):
        return col_at(sign * COLS[slot][0], sign * COLS[slot][1])

    def row_peer(slot, sign):
        return row_at(sign * ROWS[slot][0], ROWS[slot][1])

    barrier = pltpu.get_barrier_semaphore()
    peers = [(hops(COLS[s], (4, 4)), col_peer(s, 1)) for s in COL_ORDER]
    peers += [(min(o[0], 8 - o[0]), row_at(*o)) for o in ROW_PEERS]
    for _, peer in sorted(peers, key=lambda o: -o[0]):
        pl.semaphore_signal(barrier, inc=1, device_id=peer, device_id_type=MESH)

    local = [
        pltpu.make_async_copy(src, dst, lsem.at[i])
        for i, (src, dst) in enumerate((
            (scales_ref, scales_sm), (noise_ref, noise_sm), (counts_ref, counts_vm),
            (design_ref, dcol.at[OWN]), (design_ref, drow.at[0]), (targets_ref, tcol.at[OWN]), (targets_ref, trow.at[0]),
        ))
    ]
    for c in local:
        c.start()
    pl.semaphore_wait(barrier, len(COL_ORDER) + len(ROW_PEERS))

    def remote(src, dst, ssem_at, rsem, peer):
        return pltpu.make_async_remote_copy(
            src_ref=src, dst_ref=dst, send_sem=ssem.at[ssem_at], recv_sem=rsem, device_id=peer, device_id_type=MESH
        )

    def gather(*parts):
        order = [(hops(COLS[s], (4, 4)), 0, s) for s in COL_ORDER] + [(hops(ROWS[s], (8, 1)), 1, s) for s in ROW_ORDER]
        for _, is_row, s in sorted(order):
            for src, col, col_sem, row, row_sem, at in parts:
                if is_row:
                    remote(src, row.at[s], at + 1, row_sem.at[s // 2], row_peer(s, -1)).start()
                else:
                    remote(src, col.at[s], at, col_sem.at[s // 2], col_peer(s, -1)).start()

    def pair_wait(buf, sem, pair, own):
        lo, hi = 2 * pair, 2 * pair + 2
        lo = lo + 1 if lo == own else lo
        remote(buf.at[lo:hi], buf.at[lo:hi], 0, sem.at[pair], col_peer(0, 1)).wait_recv()

    def sent(ref, at):
        remote(ref, ref, at, rxs.at[0, 0], col_peer(0, 1)).wait_send()

    gather((design_ref, dcol, dcr, drow, drr, 0))
    gather((targets_ref, tcol, tcr, trow, trr, 2))

    for c in local:
        c.wait()
    dim = lax.broadcasted_iota(jnp.int32, (8, CH), 0)
    scales = jnp.zeros((8, CH), F32)
    for d in range(8):
        scales = jnp.where(dim == d, scales_sm[d], scales)
    noise = noise_sm[0] / counts_vm[...].astype(F32)
    yrow[...] = jnp.zeros_like(yrow)
    ycol[...] = jnp.zeros_like(ycol)

    def column_inputs(p):
        for h in (0, 1):
            fb[p, :, h * CH : (h + 1) * CH] = features(dcol[2 * p + h] / scales * SCALE, False).astype(BF16)

    def row_inputs(r):
        for h in (0, 1):
            fa[r, h * CH : (h + 1) * CH, :] = features(drow[2 * r + h] / scales * SCALE, True).T.astype(BF16)

    def vectors(buf, pair, out):
        for h in (0, 1):
            out[pair, :, h * CH : (h + 1) * CH] = split32(buf[2 * pair + h])

    place = {job: i for i, job in enumerate(JOBS)}

    def held(r, p):
        i = place[r, p]
        return (ka, kb)[i % 2].at[i // 2], (la, lb)[i % 2].at[i // 2]

    def tile(r, p):
        k = kernel_values(dot(fa[r], fb[p], 1, 0))
        high, low = held(r, p)
        hi = k.astype(BF16)
        high[...] = hi
        low[...] = (k - hi.astype(F32)).astype(BF16)

    def joined(values, axis):
        return jnp.concatenate(values, axis) if len(values) > 1 else values[0]

    def turn(jobs):
        @pl.when(blk >= 0)
        def _():
            for job in jobs:
                for of, to in zip(held(*job), (kt, lt)):
                    to[place[job]] = of[...].T

    def products(jobs, turned=False):
        jobs = [(is_col, own, [o for o in over if not is_col or o > 1 or own not in ONE_WAY]) for is_col, own, over in jobs]
        jobs = [job for job in jobs if job[2]]
        operands = []
        for is_col, own, over in jobs:
            vectors_of = (vc, vr)[is_col]
            at = 0 if is_col or turned else 1
            if turned and not is_col:
                high, low = ([t[place[own, o]] for o in over] for t in (kt, lt))
            else:
                high, low = ([t[...] for t in tiles] for tiles in zip(*(held(*((o, own) if is_col else (own, o))) for o in over)))
            operands.append((joined([vectors_of[o] for o in over], 1), joined(high, at), joined(low, at), at))
        first = [folded(dot(v, hi, 1, at)) for v, hi, _, at in operands]
        second = [dot(v[0:NRHS], lo, 1, at) for v, _, lo, at in operands]
        for (is_col, own, _), a, b in zip(jobs, first, second):
            (yrow, ycol)[is_col][own] += a + b

    def apart(jobs):
        @pl.when(blk >= 0)
        def _():
            products(jobs, True)

    def send_row(k, r):
        for s in (2 * r, 2 * r + 1):
            if s:
                txr[k, s - 1] = yrow[r, :, (s - 2 * r) * CH : (s - 2 * r + 1) * CH]
                remote(txr.at[k, s - 1], rxr.at[k, s - 1], 4 + 2 * k, rxs.at[k, 0], row_peer(s, 1)).start()

    def send_col(k, p):
        for s in (2 * p, 2 * p + 1):
            if s != OWN:
                i = s - (s > OWN)
                txc[k, i] = ycol[p, :, (s - 2 * p) * CH : (s - 2 * p + 1) * CH]
                remote(txc.at[k, i], rxc.at[k, i], 5 + 2 * k, rxs.at[k, 1], col_peer(s, 1)).start()

    def total(k):
        own = yrow[0, :, 0:CH] + ycol[OWN // 2, :, (OWN % 2) * CH : (OWN % 2 + 1) * CH]
        remote(rxr.at[k], rxr.at[k], 0, rxs.at[k, 0], col_peer(0, 1)).wait_recv()
        for i in range(NR - 1):
            own += rxr[k, i]
        remote(rxc.at[k], rxc.at[k], 0, rxs.at[k, 1], col_peer(0, 1)).wait_recv()
        for i in range(NC - 1):
            own += rxc[k, i]
        return own * QUAD

    rows_left = {r: sum(job[0] == r for job in JOBS) for r in range(NR // 2)}
    cols_left = {p: sum(job[1] == p for job in JOBS) for p in range(NC // 2)}
    for points, targets, values, sums in BLOCKS:
        for r in points[0]:
            pair_wait(drow, drr, r, 0)
        for p in points[1]:
            pair_wait(dcol, dcr, p, OWN)
        for r in targets[0]:
            pair_wait(trow, trr, r, 0)
        for p in targets[1]:
            pair_wait(tcol, tcr, p, OWN)

        @pl.when(blk >= 0)
        def _(points=points, targets=targets, values=values, sums=sums):
            for r in points[0]:
                row_inputs(r)
            for p in points[1]:
                column_inputs(p)
            for r in targets[0]:
                vectors(trow, r, vr)
            for p in targets[1]:
                vectors(tcol, p, vc)
            if not values:
                rows_of = {r: [q for t, q in sums if t == r] for r, _ in sums}
                cols_of = {p: [t for t, q in sums if q == p] for _, p in sums}
                products([(0, r, ps) for r, ps in rows_of.items()] + [(1, p, rs) for p, rs in cols_of.items()])
                return
            for i in range(max(len(values), len(sums))):
                if i < len(values):
                    tile(*values[i])
                if i < len(sums):
                    r, p = sums[i]
                    products([(0, r, (p,))])
                    products([(1, p, (r,))])

        for r, p in sums:
            rows_left[r] -= 1
            cols_left[p] -= 1
        for r in range(NR // 2):
            if rows_left[r] == 0:
                rows_left[r] = -1
                send_row(0, r)
        for p in range(NC // 2):
            if cols_left[p] == 0:
                cols_left[p] = -1
                send_col(0, p)

    turn(JOBS[0:20])
    sent(dcol.at[0 : NC - 1], 0)
    sent(drow.at[0 : NR - 1], 1)
    sent(tcol.at[0 : NC - 1], 2)
    sent(trow.at[0 : NR - 1], 3)
    own = tcol[OWN]
    lane = lax.broadcasted_iota(jnp.int32, (NRHS, CH), 1)
    sub = lax.broadcasted_iota(jnp.int32, (NRHS, CH), 0)
    gamma = jnp.sum(own * own, 1, keepdims=True)
    first = total(0) + noise * own

    fcol[OWN] = first
    frow[0] = first
    gather((fcol.at[OWN], fcol, fcr, frow, frr, 8))

    delta = jnp.sum(first * own, 1, keepdims=True)
    marked = jnp.where(lane == sub, gamma, 0.0) + jnp.where(lane == sub + NRHS, delta, 0.0)
    mine[0] = jnp.sum(marked, 0, keepdims=True)
    for s in COL_ORDER:
        remote(mine.at[0], stats.at[s - (s > OWN)], 10, sts.at[0], col_peer(s, 1)).start()
    first_ref[...] = first
    yrow[...] = jnp.zeros_like(yrow)
    ycol[...] = jnp.zeros_like(ycol)

    turn(JOBS[20:])

    def second(rows, cols):
        for r in rows:
            pair_wait(frow, frr, r, 0)
        for p in cols:
            pair_wait(fcol, fcr, p, OWN)
        for r in rows:
            vectors(frow, r, vr)
        for p in cols:
            vectors(fcol, p, vc)

    def met(is_col, own, others):
        return tuple(o for o in others if ((o if is_col else own) > 1 or (own if is_col else o) in HALF))

    second((), NEAR[1])
    apart([(0, r, met(0, r, NEAR[1])) for r in (1, 4, 3, 2)])
    second(NEAR[0], ())
    apart([(1, p, met(1, p, NEAR[0])) for p in (0, 7, 1)])
    second((), FAR[1])
    apart([(0, r, met(0, r, FAR[1])) for r in (1, 4)])
    send_row(1, 1)
    send_row(1, 4)
    apart([(0, r, met(0, r, FAR[1])) for r in (3, 2)])
    send_row(1, 3)
    send_row(1, 2)
    second(FAR[0], ())
    apart([(1, p, met(1, p, FAR[0])) for p in (0, 7, 1)])
    for p in (0, 7, 1):
        send_col(1, p)
    remote(stats, stats, 0, sts.at[0], col_peer(0, 1)).wait_recv()
    group = mine[0]
    for i in range(NC - 1):
        group += stats[i]
    mine[1] = group
    for i, o in enumerate(ROW_PEERS):
        remote(mine.at[1], tot.at[i], 11, sts.at[1], row_at(*o)).start()
    apart([(1, p, met(1, p, range(NR // 2))) for p in (2, 6, 3, 4, 5)] + [(0, 0, HALF)])
    for p in (2, 6, 3, 4, 5):
        send_col(1, p)
    send_row(1, 0)

    sent(txr.at[0], 4)
    sent(txc.at[0], 5)
    sent(fcol.at[0 : NC - 1], 8)
    sent(frow.at[0 : NR - 1], 9)
    sent(stats, 10)
    further_ref[...] = total(1) + noise * first_ref[...]
    remote(tot, tot, 0, sts.at[1], col_peer(0, 1)).wait_recv()
    for i in range(len(ROW_PEERS)):
        group += tot[i]
    spread = jnp.broadcast_to(group, (NRHS, CH))
    gammas = jnp.sum(jnp.where(lane == sub, spread, 0.0), 1, keepdims=True)
    deltas = jnp.sum(jnp.where(lane == sub + NRHS, spread, 0.0), 1, keepdims=True)
    alpha_ref[...] = jnp.broadcast_to(gammas / deltas, (NRHS, CH))
    sent(txr.at[1], 6)
    sent(txc.at[1], 7)
    sent(tot, 11)


def on_device(design, lengthscales, counts, noise_base, targets):
    out = jax.ShapeDtypeStruct((NRHS, CH), F32)
    vmem, hbm = (pl.BlockSpec(memory_space=m) for m in (pltpu.VMEM, pltpu.HBM))
    dma = pltpu.SemaphoreType.DMA

    def in_hbm(a):
        return pltpu.with_memory_space_constraint(a, pltpu.HBM)

    def chunks(*shape):
        return pltpu.VMEM(shape + (CH,), F32)

    alphas, first, further = pl.pallas_call(
        cg_kernel,
        out_shape=(out, out, out),
        in_specs=[hbm] * 5,
        out_specs=(vmem, vmem, vmem),
        scratch_shapes=[
            pltpu.SMEM((8,), F32), pltpu.SMEM((1,), F32), pltpu.VMEM((1, CH), jnp.int32),
            chunks(NC, 8), chunks(NR, 8), chunks(NC, NRHS), chunks(NR, NRHS), chunks(NC, NRHS), chunks(NR, NRHS),
            chunks(NC - 1, 1), chunks(len(ROW_PEERS), 1), chunks(2, 1),
            chunks(2, NR - 1, NRHS), chunks(2, NC - 1, NRHS), chunks(2, NR - 1, NRHS), chunks(2, NC - 1, NRHS),
            pltpu.VMEM((NR // 2, TILE, 64), BF16), pltpu.VMEM((NC // 2, 64, TILE), BF16),
            pltpu.VMEM((NC // 2, 2 * NRHS, TILE), BF16), pltpu.VMEM((NR // 2, 2 * NRHS, TILE), BF16),
            *[pltpu.VMEM((len(JOBS) // 2, TILE, TILE), BF16)] * 4, *[pltpu.VMEM((len(JOBS), TILE, TILE), BF16)] * 2,
            pltpu.VMEM((NR // 2, NRHS, TILE), F32), pltpu.VMEM((NC // 2, NRHS, TILE), F32),
            dma((7,)), dma((12,)), dma((NC // 2,)), dma((NR // 2,)), dma((NC // 2,)), dma((NR // 2,)),
            dma((NC // 2,)), dma((NR // 2,)), dma((2, 2)), dma((2,)),
        ],
        compiler_params=pltpu.CompilerParams(collective_id=0, has_side_effects=True, vmem_limit_bytes=48 << 20),
    )(in_hbm(design), in_hbm(lengthscales), in_hbm(counts.reshape(1, CH)), noise_base, in_hbm(targets))
    return alphas * targets, targets - alphas * first, first - alphas * further


def solution(mesh):
    both = ("blk", "grp")
    placed = (P(None, both), P(), P(both), P(), P(None, both))
    out = P(None, both)
    return jax.shard_map(on_device, mesh=mesh, in_specs=placed, out_specs=(out, out, out), check_vma=False)
```
